32 devices in a mesh: rep: 4 (over y, core), shard: 8 (over z, x).
Axes of the slice: x: 2, y: 2, z: 4, core: 2. Of those that a mesh axis runs over, the one named last changes fastest.
Arguments:
- tokens: bfloat16 [64, 1024, 512], P('rep', 'shard'), may hold values from -6 to 6
- cotangent: bfloat16 [64, 1024, 512], P('rep', 'shard'), may hold values from -6 to 6
- doc_lengths: int32 [64, 16], P('rep'), may hold values from 1 to 768, 1024 in all within a row
- attend: bfloat16 [512, 1536], P('shard'), may hold values from -0.25 to 0.25
- project: bfloat16 [512, 512], P('shard'), may hold values from -2 to 2
- widen: bfloat16 [512, 2048], P('shard'), may hold values from -0.25 to 0.25
- narrow: bfloat16 [2048, 512], P('shard'), may hold values from -0.125 to 0.125
- hidden_bias: bfloat16 [2048], P('shard'), may hold values from -3 to 3
- final_bias: bfloat16 [512], P('shard'), may hold values from -1.796875 to 1.796875
- gain_first: bfloat16 [512], P('shard'), may hold values from 0.5 to 1.5
- shift_first: bfloat16 [512], P('shard'), may hold values from -1.796875 to 1.796875
- gain_second: bfloat16 [512], P('shard'), may hold values from 0.5 to 1.5
- shift_second: bfloat16 [512], P('shard'), may hold values from -1.796875 to 1.796875
Outputs:
- block_out: float32 [64, 1024, 512], P('rep', 'shard')
- tokens_grad: float32 [64, 1024, 512], P('rep', 'shard')
- attend_grad: float32 [512, 1536], P('shard')
- project_grad: float32 [512, 512], P('shard')
- widen_grad: float32 [512, 2048], P('shard')
- narrow_grad: float32 [2048, 512], P('shard')
- hidden_bias_grad: float32 [2048], P('shard')
- final_bias_grad: float32 [512], P('shard')
- gain_first_grad: float32 [512], P('shard')
- shift_first_grad: float32 [512], P('shard')
- gain_second_grad: float32 [512], P('shard')
- shift_second_grad: float32 [512], P('shard')
The draws below stay inside these ranges and needn't reach their ends.
Inputs may be any that keep to these rules, and one draw needn't show every extreme that they name: `doc_lengths`: row s lists the lengths of the 16 documents packed in order into sequence s; they fill all 1024 positions, and the longest is 768.
All inputs are finite; a program needn't handle non-finite values.
Results may differ from the reference program's by a relative error of at most 0.017.
Values may be sent and summed in bfloat16 or wider, within the bound.
No kernel may reach another device: no remote copies, remote signals or barrier semaphores. Data moves between devices by JAX's collectives and lax.ppermute only.
A program may use at most 192 MiB of HBM per device.

```python
import math
import jax
import jax.numpy as jnp
import numpy as np
from jax import lax

HEADS = 8
D = 512
FF = 2048
SPAN = 128
NDOC = 16
LENGTH = 1024
SEQS = 64
MOST = 768


def block_scale(stream_key, extent, shards, low, largest):
    gain, own = 1.0, jax.random.fold_in(stream_key, 6)
    for axis_at, blocks in shards:
        heights = jnp.exp(jax.random.uniform(jax.random.fold_in(own, axis_at), (blocks,), jnp.float32, low / len(shards), largest / len(shards)))
        gain = gain * jnp.repeat(heights, extent[axis_at] // blocks).reshape([-1 if axis == axis_at else 1 for axis in range(len(extent))])
    return gain


def split_up(amount, total, bound, skew):
    weights = [(1 << 20) // math.isqrt(standing ** skew) + 1 for standing in range(2, amount + 1)]
    spare, given = total - bound - (amount - 1), [1] * (amount - 1)
    while spare > 0:
        candidates = [i for i in range(amount - 1) if given[i] < bound]
        whole, remaining = sum([weights[i] for i in candidates]), spare
        for i in candidates:
            more = min(bound - given[i], max(1, remaining * weights[i] // whole), spare)
            given[i] = given[i] + more
            spare = spare - more
    return np.array([bound] + given)


def ragged(own_key, number_of, total, limit, skew):
    if number_of == 2:
        one = jax.random.randint(own_key, (), max(1, total - limit), min(limit, total - 1) + 1)
        return jnp.stack([one, total - one])
    tallies = jnp.asarray(split_up(number_of, total, limit, skew), jnp.int32)
    twos = (number_of - 1) // 2
    source_of, receiver = tallies[1:1 + 2 * twos:2], tallies[2:2 + 2 * twos:2]
    slack = jnp.minimum(source_of - 1, limit - receiver)
    passed = jax.random.randint(jax.random.fold_in(own_key, 1), (twos,), 0, 1 << 20) % (slack + 1)
    tallies = tallies.at[1:1 + 2 * twos:2].set(source_of - passed).at[2:2 + 2 * twos:2].set(receiver + passed)
    return tallies[jax.random.permutation(jax.random.fold_in(own_key, 2), number_of)]


def gaussian(key, shape, scale, most, split=(), kind=jnp.bfloat16):
    loudness = block_scale(key, shape, split, -0.22, 0.18) if split else 1.0
    drawn = jax.random.normal(key, shape, jnp.float32) * scale * loudness
    return jnp.minimum(jnp.maximum(drawn, -most), most).astype(kind)


def setup_inputs(seed: int = 0) -> dict:
    seeds = jax.random.split(jax.random.key(seed), 14)
    tokens = gaussian(seeds[0], (SEQS, LENGTH, D), 1.0, 6.0, ((0, 4), (1, 8)))
    cotangent = gaussian(seeds[1], (SEQS, LENGTH, D), 1.0, 6.0, ((0, 4), (1, 8)))
    doc_lengths = jax.vmap(lambda own: ragged(own, NDOC, LENGTH, MOST, 2))(jax.random.split(seeds[2], SEQS)).reshape((SEQS, NDOC)).astype(jnp.int32)
    attend = gaussian(seeds[3], (D, 3 * D), D ** -0.5, 0.25, ((0, 8),))
    project = gaussian(seeds[4], (D, D), (max(D // 64, 1)) ** -0.5, 2.0, ((0, 8),))
    widen = gaussian(seeds[5], (D, FF), D ** -0.5, 0.25, ((0, 8),))
    narrow = gaussian(seeds[6], (FF, D), FF ** -0.5, 0.125, ((0, 8),))
    hidden_bias = gaussian(seeds[7], (FF,), 0.5, 3.0, ((0, 8),))
    final_bias = gaussian(seeds[8], (D,), 0.3, 1.796875, ((0, 8),))
    gain_first = jnp.clip(1.0 + 0.1 * jax.random.normal(seeds[9], (D,), jnp.float32), 0.5, 1.5).astype(jnp.bfloat16)
    shift_first = gaussian(seeds[10], (D,), 0.3, 1.796875, ((0, 8),))
    gain_second = jnp.clip(1.0 + 0.1 * jax.random.normal(seeds[11], (D,), jnp.float32), 0.5, 1.5).astype(jnp.bfloat16)
    shift_second = gaussian(seeds[12], (D,), 0.3, 1.796875, ((0, 8),))
    return {"tokens": tokens, "cotangent": cotangent, "doc_lengths": doc_lengths, "attend": attend, "project": project, "widen": widen, "narrow": narrow, "hidden_bias": hidden_bias, "final_bias": final_bias, "gain_first": gain_first, "shift_first": shift_first, "gain_second": gain_second, "shift_second": shift_second}


epsilon = 1e-05
masked = -1e+30
highest = lax.Precision.HIGHEST

@jax.custom_vjp
def low(v):
    return lax.optimization_barrier(v.astype(jnp.bfloat16)).astype(jnp.float32)

@jax.custom_vjp
def low_back(v):
    return v

def low_keep(v):
    return (low(v), None)

def low_pass(kept, grad):
    return (grad,)

def back_keep(v):
    return (v, None)

def back_low(kept, grad):
    return (low(grad),)
low.defvjp(low_keep, low_pass)
low_back.defvjp(back_keep, back_low)

def layer_norm(values, scale_gain, shift_add):
    center = values - lax.optimization_barrier(jnp.mean(values, axis=-1, keepdims=True))
    variance = lax.optimization_barrier(jnp.mean(center * center, axis=-1, keepdims=True))
    return center * lax.rsqrt(variance + epsilon) * scale_gain + shift_add

def doc_layout(lengths, positions, span_rows, span_count):
    doc_ends = jnp.cumsum(lengths, axis=-1, dtype=jnp.int32)
    doc_starts = doc_ends - lengths
    segment = lax.optimization_barrier(jnp.sum((positions[None, :, None] >= doc_ends[:, None, :]).astype(jnp.int32), axis=-1, dtype=jnp.int32))
    span_last = (jnp.arange(span_count, dtype=jnp.int32) + 1) * span_rows - 1
    last_doc = lax.optimization_barrier(jnp.sum((span_last[None, :, None] >= doc_ends[:, None, :]).astype(jnp.int32), axis=-1, dtype=jnp.int32))
    picked = last_doc[:, :, None] == jnp.arange(lengths.shape[-1], dtype=jnp.int32)[None, None, :]
    last_start = lax.optimization_barrier(jnp.sum(jnp.where(picked, doc_starts[:, None, :], 0), axis=-1, dtype=jnp.int32))
    counts = jnp.minimum(span_rows, span_last[None, :] + 1 - last_start)
    return (segment, last_doc, counts)

def score_bias(segment, last_doc, counts, position_span):
    span_rows = segment.shape[1]
    row_ids = jnp.arange(span_rows, dtype=jnp.int32)
    causal = row_ids[None, :, None] >= row_ids[None, None, :]
    same_doc = segment[:, :, None] == segment[:, None, :]
    direct = jnp.where(causal & same_doc, 0.0, masked)
    earlier = jnp.arange(counts.shape[1], dtype=jnp.int32)[None, None, :] < position_span
    doc_match = last_doc[:, None, :] == segment[:, :, None]
    pooled_bias = jnp.where(earlier & doc_match, jnp.log(counts.astype(jnp.float32))[:, None, :], masked)
    return jnp.concatenate([direct.astype(jnp.float32), pooled_bias.astype(jnp.float32)], axis=-1)

def gelu_exact(values):
    return jax.nn.gelu(values, approximate=False)

def forward(params, inputs, lengths):
    attend, project, widen, narrow, hidden_bias, final_bias, gain_first, shift_first, gain_second, shift_second = params
    total_rows = inputs.shape[0]
    span_count = total_rows // SPAN
    model_width = inputs.shape[1]
    head_size = model_width // HEADS
    positions = jnp.arange(total_rows, dtype=jnp.int32)
    segment, last_doc, counts = doc_layout(lengths[None, :], positions, SPAN, span_count)
    segment = segment.reshape(span_count, SPAN)
    last_row = jnp.broadcast_to(last_doc, (span_count, span_count))
    count_row = jnp.broadcast_to(counts, (span_count, span_count))
    bias_all = score_bias(segment, last_row, count_row, jnp.arange(span_count, dtype=jnp.int32)[:, None, None])
    normed_one = low(layer_norm(inputs, gain_first, shift_first))
    qkv_all = low(low_back(jnp.dot(normed_one, attend, precision=highest)))
    qkv_spans = qkv_all.reshape(span_count, SPAN, 3 * model_width)
    member = (segment == last_doc[0][:, None]).astype(jnp.float32)
    pooled = low(jnp.einsum('ct,ctd->cd', member, qkv_spans[:, :, model_width:], precision=highest) / counts[0][:, None].astype(jnp.float32))
    queries = qkv_spans[:, :, :model_width].reshape(span_count, SPAN, HEADS, head_size)
    key_all = jnp.concatenate([qkv_spans[:, :, model_width:2 * model_width], jnp.broadcast_to(pooled[None, :, :model_width], (span_count, span_count, model_width))], axis=1)
    value_all = jnp.concatenate([qkv_spans[:, :, 2 * model_width:], jnp.broadcast_to(pooled[None, :, model_width:], (span_count, span_count, model_width))], axis=1)
    key_all = key_all.reshape(span_count, SPAN + span_count, HEADS, head_size)
    value_all = value_all.reshape(span_count, SPAN + span_count, HEADS, head_size)
    scores = low_back(jnp.einsum('bqhe,bkhe->bhqk', queries, key_all, precision=highest) * head_size ** (-0.5) + bias_all[:, None])
    attn_probs = low(jax.nn.softmax(scores, axis=-1))
    attn_out = jnp.einsum('bhqk,bkhe->bqhe', attn_probs, value_all, precision=highest).reshape(total_rows, model_width)
    attn_low = low(low_back(attn_out))
    residual = inputs + low_back(jnp.dot(attn_low, project, precision=highest))
    normed_two = low(layer_norm(residual, gain_second, shift_second))
    pre_act = low_back(jnp.dot(normed_two, widen, precision=highest) + hidden_bias)
    activation = low(gelu_exact(pre_act))
    return residual + jnp.dot(activation, narrow, precision=highest) + final_bias

def reference(tokens, cotangent, doc_lengths, attend, project, widen, narrow, hidden_bias, final_bias, gain_first, shift_first, gain_second, shift_second):
    params = tuple((weight.astype(jnp.float32) for weight in (attend, project, widen, narrow, hidden_bias, final_bias, gain_first, shift_first, gain_second, shift_second)))
    inputs = tokens.astype(jnp.float32)
    cot_rows = cotangent.astype(jnp.float32)

    def per_sequence(grad_sum, sequence_item):
        seq_in, seq_cot, seq_lengths = sequence_item
        result, pull_back = jax.vjp(lambda weights, rows: forward(weights, rows, seq_lengths), params, seq_in)
        weight_grads, input_grad = pull_back(seq_cot)
        return (tuple((left + right for left, right in zip(grad_sum, weight_grads))), (result, input_grad))
    zero_grads = tuple((jnp.zeros_like(weight) for weight in params))
    grad_sum, (block_out, tokens_grad) = lax.scan(per_sequence, zero_grads, (inputs, cot_rows, doc_lengths))
    return (block_out, tokens_grad, grad_sum[0], grad_sum[1], grad_sum[2], grad_sum[3], grad_sum[4], grad_sum[5], grad_sum[6], grad_sum[7], grad_sum[8], grad_sum[9])
```

```python
import functools

import jax
import jax.numpy as jnp
from jax import lax
from jax.experimental import pallas as pl
from jax.experimental.pallas import tpu as pltpu
from jax.sharding import PartitionSpec as P

HEADS = 8
epsilon = 1e-05
masked = -1e30
F32 = jnp.float32
BF = jnp.bfloat16
MIB = 1 << 20


def dot(a, b):
    return jnp.dot(a, b, preferred_element_type=F32)


def dot_nt(a, b):
    return lax.dot_general(a, b, (((1,), (1,)), ((), ())), preferred_element_type=F32)


def dot_tn(a, b):
    return lax.dot_general(a, b, (((0,), (0,)), ((), ())), preferred_element_type=F32)


def normed(v):
    center = v - jnp.mean(v, axis=-1, keepdims=True)
    rstd = lax.rsqrt(jnp.mean(center * center, axis=-1, keepdims=True) + epsilon)
    return center * rstd, rstd


def norm_back(e, n, rstd):
    return rstd * (
        e - jnp.mean(e, axis=-1, keepdims=True) - n * jnp.mean(e * n, axis=-1, keepdims=True)
    )


def two_heads_lanes(t):
    half = t.shape[0] // 2
    zero = jnp.zeros((half, t.shape[1]), t.dtype)
    left = jnp.concatenate([t[:half], zero], axis=0)
    right = jnp.concatenate([zero, t[half:]], axis=0)
    return jnp.concatenate([left, right], axis=1)


def two_heads_rows(a):
    first = lax.broadcasted_iota(jnp.int32, a.shape, 1) < a.shape[1] // 2
    zero = jnp.zeros_like(a)
    return jnp.concatenate([jnp.where(first, a, zero), jnp.where(first, zero, a)], axis=0)


def diagonal(t):
    rows, cols = t.shape[0] // 2, t.shape[1] // 2
    return jnp.concatenate([t[:rows, :cols], t[rows:, cols:]], axis=0)


def span_bias(doc_from, pooled):
    span = doc_from.shape[1]
    key = lax.broadcasted_iota(jnp.int32, (span, span), 0)
    query = lax.broadcasted_iota(jnp.int32, (span, span), 1)
    direct = jnp.where((key >= doc_from) & (key <= query), 0.0, masked).astype(F32)
    both = jnp.concatenate([direct, pooled], axis=0)
    return jnp.concatenate([both, both], axis=1)


def copies(meta, sizes, pieces, place, sems):
    zs, xs = sizes
    z, x, core = meta[0], meta[1], meta[2]
    started = []
    for which in range(2):
        half = core if which == 0 else 1 - core
        for kx in range(xs):
            ref = pieces[which * xs + kx]
            for kz in range(zs):
                shard = lax.rem(z - kz + zs, zs) * xs + lax.rem(x - kx + xs, xs)
                for src, dst in place(ref, kz, shard, half):
                    copy = pltpu.make_async_copy(src, dst, sems.at[len(started)])
                    copy.start()
                    started.append(copy)
    for copy in started:
        copy.wait()


def pool_kernel(rel_ref, x_ref, out_ref, *, seqs, span):
    n, _ = normed(x_ref[...].astype(F32))
    for i in range(seqs):
        first = rel_ref[pl.program_id(0) * seqs + i]
        row = lax.broadcasted_iota(jnp.int32, (span, n.shape[1]), 0)
        part = jnp.where(row >= first, n[i * span : (i + 1) * span], 0.0)
        count = jnp.full((1, 1), span - first, jnp.int32).astype(F32)
        out_ref[i] = jnp.sum(part, axis=0, keepdims=True) / count


def attend_kernel(meta, *refs, sizes, seqs, span, npieces, rps):
    x_ref, gain_ref, shift_ref, pool_ref, from_ref, pbias_ref = refs[:6]
    pieces = refs[6 : 6 + npieces]
    w_ref, qkv_ref, o_ref, lse_ref, sems = refs[6 + npieces :]
    width = x_ref.shape[1]
    nh = w_ref.shape[1] // 2

    @pl.when(pl.program_id(0) == 0)
    def _():
        def place(ref, kz, shard, half):
            yield (
                ref.at[pl.ds(kz * rps, rps), :],
                w_ref.at[
                    pl.ds(pl.multiple_of(shard * rps, rps), rps),
                    pl.ds(pl.multiple_of(half * nh, 128), nh),
                ],
            )

        copies(meta, sizes, pieces, place, sems)

    gain, shift = gain_ref[...], shift_ref[...]
    n, _ = normed(x_ref[...].astype(F32))
    h = (n * gain + shift).astype(BF)
    qkv = dot(h, w_ref[...]).astype(BF)
    q = qkv[:, :width] * jnp.asarray((width // HEADS) ** -0.5, BF)
    qkv_ref[:, :width] = q
    qkv_ref[:, width:] = qkv[:, width:]
    cp = pool_ref.shape[1]
    pooled_h = pool_ref[...].astype(F32).reshape(seqs * cp, width) * gain + shift
    kvb = dot(pooled_h.astype(BF), w_ref[:, width:]).astype(BF)
    for s in range(seqs):
        rows = slice(s * span, (s + 1) * span)
        prow = slice(s * cp, (s + 1) * cp)
        bias = span_bias(from_ref[s], pbias_ref[s])
        for p in range(HEADS // 2):
            col = slice(p * 128, (p + 1) * 128)
            kcol = slice(width + p * 128, width + (p + 1) * 128)
            vcol = slice(2 * width + p * 128, 2 * width + (p + 1) * 128)
            keys = jnp.concatenate([qkv[rows, kcol], kvb[prow, col]], axis=0)
            vals = jnp.concatenate(
                [qkv[rows, vcol], kvb[prow, width + p * 128 : width + (p + 1) * 128]], axis=0
            )
            scores = dot(keys, two_heads_lanes(q[rows, col].T)) + bias
            top = jnp.max(scores, axis=0, keepdims=True)
            e = jnp.exp(scores - top)
            total = jnp.sum(e, axis=0, keepdims=True)
            prob = (e * (1.0 / total)).astype(BF)
            lse_ref[s, p : p + 1, :] = top + jnp.log(total)
            out = diagonal(dot_tn(vals, prob)).astype(BF)
            o_ref[rows, col] = out.T


def ffn_kernel(meta, *refs, sizes, npieces, rps, chunk):
    o_ref, x_ref, y_ref, hb_ref, fb_ref, gain_ref, shift_ref = refs[:7]
    pieces = refs[7 : 7 + npieces]
    (
        out_ref,
        dr_ref,
        keep_ref,
        send_ref,
        wp_ref,
        vec_ref,
        w1_ref,
        w2_ref,
        acc1_ref,
        acc2_ref,
        accp_ref,
        sems,
    ) = refs[7 + npieces :]
    width, hidden = w1_ref.shape
    per = hidden // width
    ph, wh = width // 2, hidden // 2
    step = pl.program_id(0)

    @pl.when(step == 0)
    def _():
        def place(ref, kz, shard, half):
            src = pl.ds(kz * rps, rps)
            row = pl.ds(pl.multiple_of(shard * rps, rps), rps)
            yield (
                ref.at[src, pl.ds(0, ph)],
                wp_ref.at[row, pl.ds(pl.multiple_of(half * ph, 128), ph)],
            )
            yield (
                ref.at[src, pl.ds(ph, wh)],
                w1_ref.at[row, pl.ds(pl.multiple_of(half * wh, 128), wh)],
            )
            for j in range(per // 2):
                at = (shard * per + half * (per // 2) + j) * rps
                yield (
                    ref.at[src, pl.ds(ph + wh + j * width, width)],
                    w2_ref.at[pl.ds(pl.multiple_of(at, rps), rps), :],
                )

        copies(meta, sizes, pieces, place, sems)
        acc1_ref[...] = jnp.zeros_like(acc1_ref)
        acc2_ref[...] = jnp.zeros_like(acc2_ref)
        accp_ref[...] = jnp.zeros_like(accp_ref)
        vec_ref[...] = jnp.zeros_like(vec_ref)

    o, y = o_ref[...], y_ref[...]
    r1 = x_ref[...].astype(F32) + dot(o, wp_ref[...])
    n, rstd = normed(r1)
    h = (n * gain_ref[...] + shift_ref[...]).astype(BF)
    ht = h.T
    out = r1 + fb_ref[...]
    dh = jnp.zeros_like(r1)
    for j in range(hidden // chunk):
        at = slice(j * chunk, (j + 1) * chunk)
        u = dot(h, w1_ref[:, at]) + hb_ref[:, at]
        da = dot_nt(y, w2_ref[at, :])
        cdf = 0.5 + 0.5 * lax.erf(u * 0.7071067811865476)
        pdf = jnp.exp(u * u * -0.5) * 0.3989422804014327
        a = (u * cdf).astype(BF)
        du = (da * (cdf + u * pdf)).astype(BF)
        out += dot(a, w2_ref[at, :])
        dh += dot_nt(du, w1_ref[:, at])
        acc1_ref[:, at] += dot(ht, du)
        acc2_ref[at, :] += dot_tn(a, y)
        vec_ref[0:1, at] += jnp.sum(du.astype(F32), axis=0, keepdims=True)
    out_ref[...] = out
    yf = y.astype(F32)
    dr = yf + norm_back(dh * gain_ref[...], n, rstd)
    dr_ref[...] = dr
    accp_ref[...] += dot_tn(o, dr.astype(BF))
    vec_ref[1:2, :width] += jnp.sum(yf, axis=0, keepdims=True)
    vec_ref[2:3, :width] += jnp.sum(dh * n, axis=0, keepdims=True)
    vec_ref[3:4, :width] += jnp.sum(dh, axis=0, keepdims=True)

    @pl.when(step == pl.num_programs(0) - 1)
    def _():
        for which, ref in ((0, keep_ref), (1, send_ref)):
            half = meta[2] if which == 0 else 1 - meta[2]
            pcol = pl.ds(pl.multiple_of(half * ph, 128), ph)
            ref[:, :ph] = accp_ref[:, pcol].astype(BF)
            ref[:, ph : ph + wh] = acc1_ref[:, pl.ds(pl.multiple_of(half * wh, 128), wh)].astype(BF)
            for shard in range(width // rps):
                for j in range(per):
                    at = (shard * per + j) * rps
                    ref[shard * rps : (shard + 1) * rps, ph + wh + j * ph : ph + wh + (j + 1) * ph] = (
                        acc2_ref[at : at + rps, pcol].astype(BF)
                    )


def back_kernel(
    meta,
    dr_ref,
    x_ref,
    qkv_ref,
    lse_ref,
    w_ref,
    wp_ref,
    gain_ref,
    shift_ref,
    pool_ref,
    from_ref,
    pbias_ref,
    part_ref,
    dpool_ref,
    keep_ref,
    send_ref,
    vec_ref,
    acc_ref,
    dqkv_ref,
    dkvb_ref,
    *,
    seqs,
    span,
):
    width = x_ref.shape[1]
    scale = (width // HEADS) ** -0.5
    step = pl.program_id(0)

    @pl.when(step == 0)
    def _():
        acc_ref[...] = jnp.zeros_like(acc_ref)
        vec_ref[...] = jnp.zeros_like(vec_ref)

    gain, shift = gain_ref[...], shift_ref[...]
    cp = pool_ref.shape[1]
    pool = pool_ref[...].astype(F32).reshape(seqs * cp, width)
    pooled_h = (pool * gain + shift).astype(BF)
    kvb = dot(pooled_h, w_ref[:, width:]).astype(BF)
    dr = dr_ref[...]
    do = dot_nt(dr.astype(BF), wp_ref[...]).astype(BF)
    for s in range(seqs):
        rows = slice(s * span, (s + 1) * span)
        prow = slice(s * cp, (s + 1) * cp)
        bias = span_bias(from_ref[s], pbias_ref[s])
        for p in range(HEADS // 2):
            col = slice(p * 128, (p + 1) * 128)
            kcol = slice(width + p * 128, width + (p + 1) * 128)
            vcol = slice(2 * width + p * 128, 2 * width + (p + 1) * 128)
            v2col = slice(width + p * 128, width + (p + 1) * 128)
            q = qkv_ref[rows, col]
            g = do[rows, col]
            keys = jnp.concatenate([qkv_ref[rows, kcol], kvb[prow, col]], axis=0)
            vals = jnp.concatenate([qkv_ref[rows, vcol], kvb[prow, v2col]], axis=0)
            scores = dot(keys, two_heads_lanes(q.T)) + bias
            prob = jnp.exp(scores - lse_ref[s, p : p + 1, :])
            dprob = dot(vals, two_heads_lanes(g.T))
            weighted = prob * dprob
            ds = (weighted - prob * jnp.sum(weighted, axis=0, keepdims=True)).astype(BF)
            dq = (diagonal(dot_tn(keys, ds)) * scale).astype(BF)
            dk = dot(ds, two_heads_rows(q)).astype(BF)
            dv = dot(prob.astype(BF), two_heads_rows(g)).astype(BF)
            dqkv_ref[rows, col] = dq.T
            dqkv_ref[rows, kcol] = dk[:span]
            dqkv_ref[rows, vcol] = dv[:span]
            dkvb_ref[prow, col] = dk[span:]
            dkvb_ref[prow, v2col] = dv[span:]
    n, rstd = normed(x_ref[...].astype(F32))
    h = (n * gain + shift).astype(BF)
    dqkv, dkvb = dqkv_ref[...], dkvb_ref[...]
    acc_ref[...] += dot_tn(h, dqkv)
    acc_ref[:, width:] += dot_tn(pooled_h, dkvb)
    dh = dot_nt(dqkv, w_ref[...])
    dpool = dot_nt(dkvb, w_ref[:, width:])
    dpool_ref[...] = dpool.astype(BF).reshape(seqs, cp, width)
    vec_ref[0:1, :] += jnp.sum(dh * n, axis=0, keepdims=True) + jnp.sum(
        dpool * pool, axis=0, keepdims=True
    )
    vec_ref[1:2, :] += jnp.sum(dh, axis=0, keepdims=True) + jnp.sum(dpool, axis=0, keepdims=True)
    part_ref[...] = dr + norm_back(dh * gain, n, rstd)

    @pl.when(step == pl.num_programs(0) - 1)
    def _():
        nh = acc_ref.shape[1] // 2
        for which, ref in ((0, keep_ref), (1, send_ref)):
            half = meta[2] if which == 0 else 1 - meta[2]
            ref[...] = acc_ref[:, pl.ds(pl.multiple_of(half * nh, 128), nh)].astype(BF)


def last_kernel(rel_ref, part_ref, x_ref, dpool_ref, gain_ref, out_ref, *, seqs, span):
    n, rstd = normed(x_ref[...].astype(F32))
    for i in range(seqs):
        first = rel_ref[pl.program_id(0) * seqs + i]
        rows = slice(i * span, (i + 1) * span)
        count = jnp.full((1, 1), span - first, jnp.int32).astype(F32)
        share = dpool_ref[i] / count * gain_ref[...]
        row = lax.broadcasted_iota(jnp.int32, (span, n.shape[1]), 0)
        e = jnp.where(row >= first, share, 0.0)
        out_ref[rows, :] = part_ref[rows, :] + norm_back(e, n[rows], rstd[rows])


def params(mib):
    return pltpu.CompilerParams(
        dimension_semantics=("arbitrary",), vmem_limit_bytes=mib * MIB
    )


def local(
    tokens,
    cotangent,
    doc_lengths,
    attend,
    project,
    widen,
    narrow,
    hidden_bias,
    final_bias,
    gain_first,
    shift_first,
    gain_second,
    shift_second,
    *,
    sizes,
):
    zs, xs, ys, cs = sizes
    nshard = zs * xs
    seq_count, span, width = tokens.shape
    rows = seq_count * span
    hidden = widen.shape[1]
    rps = attend.shape[0]
    rep, shard = lax.axis_index("rep"), lax.axis_index("shard")
    z, x, y, core = shard // xs, shard % xs, rep // cs, rep % cs
    meta = jnp.stack([z, x, core]).astype(jnp.int32)

    def send(a, dz=0, dx=0, dy=0, dc=0):
        perm = []
        for r in range(ys * cs):
            for s in range(nshard):
                r2 = (r // cs + dy) % ys * cs + (r % cs + dc) % cs
                s2 = (s // xs + dz) % zs * xs + (s % xs + dx) % xs
                perm.append((r * nshard + s, r2 * nshard + s2))
        return lax.ppermute(a, ("rep", "shard"), perm)

    def gather(a):
        col = jnp.concatenate([a] + [send(a, dz=k) for k in range(1, zs)], axis=0)
        return [col] + [send(col, dx=k) for k in range(1, xs)]

    def gather_halves(a):
        mine = gather(a)
        return mine + [send(m, dc=1) for m in mine]

    ndoc = doc_lengths.shape[1]
    upto = jnp.arange(ndoc)[:, None] <= jnp.arange(ndoc)[None, :]
    ends = jnp.sum(jnp.where(upto[None], doc_lengths[:, :, None], 0), axis=1, dtype=jnp.int32)
    starts = ends - doc_lengths
    base = shard * span
    positions = base + jnp.arange(span, dtype=jnp.int32)
    segment = jnp.sum(
        (positions[None, :, None] >= ends[:, None, :]).astype(jnp.int32), axis=-1, dtype=jnp.int32
    )

    def start_at(at):
        before = starts[:, None, :] <= at[..., None]
        return jnp.max(jnp.where(before, starts[:, None, :], 0), axis=-1)

    doc_from = (start_at(positions[None, :]) - base)[:, None, :]
    slot = jnp.arange(nshard, dtype=jnp.int32)
    slot_span = (z - slot % zs + zs) % zs * xs + (x - slot // zs + xs) % xs
    slot_last = slot_span * span + span - 1
    last_doc = jnp.sum(
        (slot_last[None, :, None] >= ends[:, None, :]).astype(jnp.int32), axis=-1, dtype=jnp.int32
    )
    counts = jnp.minimum(span, slot_last[None, :] + 1 - start_at(slot_last[None, :]))
    seen = (slot_span[None, :, None] < shard) & (last_doc[:, :, None] == segment[:, None, :])
    pbias = jnp.where(seen, jnp.log(counts.astype(F32))[:, :, None], masked)
    cp = max(16, -(-nshard // 16) * 16)
    pbias = jnp.pad(pbias, ((0, 0), (0, cp - nshard), (0, 0)), constant_values=masked)
    rel = span - counts[:, 0]

    nh = attend.shape[1] // 2
    attend_parts = gather_halves(lax.dynamic_slice_in_dim(attend, core * nh, nh, 1))
    x2 = tokens.reshape(rows, width)
    y2 = cotangent.reshape(rows, width)
    smem = pl.BlockSpec(memory_space=pltpu.SMEM)
    hbm = pl.BlockSpec(memory_space=pl.ANY)
    pool_seqs = 4
    pool = pl.pallas_call(
        functools.partial(pool_kernel, seqs=pool_seqs, span=span),
        grid=(seq_count // pool_seqs,),
        in_specs=[smem, pl.BlockSpec((pool_seqs * span, width), lambda i: (i, 0))],
        out_specs=pl.BlockSpec((pool_seqs, 1, width), lambda i: (i, 0, 0)),
        out_shape=jax.ShapeDtypeStruct((seq_count, 1, width), F32),
        compiler_params=params(16),
        name="pool",
    )(rel, x2)
    small = jnp.concatenate(
        [hidden_bias, final_bias, gain_first, shift_first, gain_second, shift_second]
    )
    nsmall = small.shape[0]
    srows = -(-nsmall // width)
    small = jnp.pad(small, (0, srows * width - nsmall)).reshape(srows, width)
    packed = jnp.concatenate([pool.reshape(seq_count, width).astype(BF), small], axis=0)
    slots = jnp.concatenate(gather(packed), axis=0).reshape(nshard, seq_count + srows, width)
    pool_all = jnp.transpose(slots[:, :seq_count], (1, 0, 2))
    pool_all = jnp.pad(pool_all, ((0, 0), (0, cp - nshard), (0, 0)))
    which = slot_span[None, :] == jnp.arange(nshard)[:, None]
    values = slots[:, seq_count:].reshape(nshard, srows * width).astype(F32)
    values = jnp.sum(jnp.where(which[:, :, None], values[None], 0.0), axis=1)
    hs = hidden_bias.shape[0]
    hidden_all = values[:, :hs].reshape(1, hidden)
    final_all, gain1, shift1, gain2, shift2 = (
        values[:, hs + i * rps : hs + (i + 1) * rps].reshape(1, width) for i in range(5)
    )

    per = hidden // width
    ph, wh = width // 2, hidden // 2
    nhalf = lax.dynamic_slice_in_dim(narrow, core * (narrow.shape[0] // 2), narrow.shape[0] // 2, 0)
    ffn_half = jnp.concatenate(
        [
            lax.dynamic_slice_in_dim(project, core * ph, ph, 1),
            lax.dynamic_slice_in_dim(widen, core * wh, wh, 1),
        ]
        + [nhalf[j * rps : (j + 1) * rps] for j in range(per // 2)],
        axis=1,
    )
    ffn_parts = gather_halves(ffn_half)

    seqs = 2
    row_spec = lambda n, w: pl.BlockSpec((n, w), lambda i, m: (i, 0))
    all_spec = lambda a, b: pl.BlockSpec((a, b), lambda i, m: (0, 0))
    seq_spec = lambda n, a, b: pl.BlockSpec((n, a, b), lambda i, m: (i, 0, 0))
    npieces = 2 * xs
    w_all, qkv, o, lse = pl.pallas_call(
        functools.partial(
            attend_kernel, sizes=(zs, xs), seqs=seqs, span=span, npieces=npieces, rps=rps
        ),
        grid_spec=pltpu.PrefetchScalarGridSpec(
            num_scalar_prefetch=1,
            grid=(seq_count // seqs,),
            in_specs=[
                row_spec(seqs * span, width),
                all_spec(1, width),
                all_spec(1, width),
                seq_spec(seqs, cp, width),
                seq_spec(seqs, 1, span),
                seq_spec(seqs, cp, span),
            ]
            + [hbm] * npieces,
            out_specs=[
                all_spec(width, 3 * width),
                row_spec(seqs * span, 3 * width),
                row_spec(seqs * span, width),
                seq_spec(seqs, HEADS // 2, 2 * span),
            ],
            scratch_shapes=[pltpu.SemaphoreType.DMA((2 * nshard,))],
        ),
        out_shape=[
            jax.ShapeDtypeStruct((width, 3 * width), BF),
            jax.ShapeDtypeStruct((rows, 3 * width), BF),
            jax.ShapeDtypeStruct((rows, width), BF),
            jax.ShapeDtypeStruct((seq_count, HEADS // 2, 2 * span), F32),
        ],
        compiler_params=params(40),
        name="attention",
    )(meta, x2, gain1, shift1, pool_all, doc_from, pbias, *attend_parts)

    tile = 256
    packet = ph + wh + per * ph
    block_out, dr, keep_f, send_f, wp_all, vec_f = pl.pallas_call(
        functools.partial(ffn_kernel, sizes=(zs, xs), npieces=npieces, rps=rps, chunk=512),
        grid_spec=pltpu.PrefetchScalarGridSpec(
            num_scalar_prefetch=1,
            grid=(rows // tile,),
            in_specs=[
                row_spec(tile, width),
                row_spec(tile, width),
                row_spec(tile, width),
                all_spec(1, hidden),
                all_spec(1, width),
                all_spec(1, width),
                all_spec(1, width),
            ]
            + [hbm] * npieces,
            out_specs=[
                row_spec(tile, width),
                row_spec(tile, width),
                all_spec(width, packet),
                all_spec(width, packet),
                all_spec(width, width),
                all_spec(8, hidden),
            ],
            scratch_shapes=[
                pltpu.VMEM((width, hidden), BF),
                pltpu.VMEM((hidden, width), BF),
                pltpu.VMEM((width, hidden), F32),
                pltpu.VMEM((hidden, width), F32),
                pltpu.VMEM((width, width), F32),
                pltpu.SemaphoreType.DMA((2 * nshard * (2 + per // 2),)),
            ],
        ),
        out_shape=[
            jax.ShapeDtypeStruct((rows, width), F32),
            jax.ShapeDtypeStruct((rows, width), F32),
            jax.ShapeDtypeStruct((width, packet), BF),
            jax.ShapeDtypeStruct((width, packet), BF),
            jax.ShapeDtypeStruct((width, width), BF),
            jax.ShapeDtypeStruct((8, hidden), F32),
        ],
        compiler_params=params(56),
        name="ffn",
    )(meta, o, x2, y2, hidden_all, final_all, gain2, shift2, *ffn_parts)

    seqs = 4
    part, dpool, keep_a, send_a, vec_a = pl.pallas_call(
        functools.partial(back_kernel, seqs=seqs, span=span),
        grid_spec=pltpu.PrefetchScalarGridSpec(
            num_scalar_prefetch=1,
            grid=(seq_count // seqs,),
            in_specs=[
                row_spec(seqs * span, width),
                row_spec(seqs * span, width),
                row_spec(seqs * span, 3 * width),
                seq_spec(seqs, HEADS // 2, 2 * span),
                all_spec(width, 3 * width),
                all_spec(width, width),
                all_spec(1, width),
                all_spec(1, width),
                seq_spec(seqs, cp, width),
                seq_spec(seqs, 1, span),
                seq_spec(seqs, cp, span),
            ],
            out_specs=[
                row_spec(seqs * span, width),
                seq_spec(seqs, cp, width),
                all_spec(width, 3 * width // 2),
                all_spec(width, 3 * width // 2),
                all_spec(8, width),
            ],
            scratch_shapes=[
                pltpu.VMEM((width, 3 * width), F32),
                pltpu.VMEM((seqs * span, 3 * width), BF),
                pltpu.VMEM((seqs * cp, 2 * width), BF),
            ],
        ),
        out_shape=[
            jax.ShapeDtypeStruct((rows, width), F32),
            jax.ShapeDtypeStruct((seq_count, cp, width), BF),
            jax.ShapeDtypeStruct((width, 3 * width // 2), BF),
            jax.ShapeDtypeStruct((width, 3 * width // 2), BF),
            jax.ShapeDtypeStruct((8, width), F32),
        ],
        compiler_params=params(56),
        name="back",
    )(meta, dr, x2, qkv, lse, w_all, wp_all, gain1, shift1, pool_all, doc_from, pbias)

    def add(parts, kind):
        total = parts[0].astype(F32)
        for p in parts[1:]:
            total = total + p.astype(F32)
        return total.astype(kind)

    def reduce_packet(keep, sent):
        kind = keep.dtype
        part = add([keep, send(sent, dc=1)], kind)
        n = part.shape[1] // ys
        k = part.shape[0] // nshard
        view = part.reshape(zs, xs, k, ys * n)

        def corner(dx, dy):
            at = (0, (x + dx) % xs, 0, (y + dy) % ys * n)
            return lax.dynamic_slice(view, at, (zs, 1, k, n)).reshape(zs * k, n)

        part = add(
            [
                send(corner(dx, dy), dx=dx, dy=dy) if dx or dy else corner(0, 0)
                for dx in range(xs)
                for dy in range(ys)
            ],
            kind,
        )
        level = lambda dz: lax.dynamic_slice_in_dim(part, (z + dz) % zs * k, k, 0)
        part = add([send(level(dz), dz=dz) if dz else level(0) for dz in range(zs)], kind)
        total = []
        found = {
            (dy, dc): send(part, dy=dy, dc=dc) if dy or dc else part
            for dy in range(ys)
            for dc in range(cs)
        }
        for at in range(ys * cs):
            picked = jnp.zeros(part.shape, F32)
            for (dy, dc), piece in found.items():
                mine = ((y - dy + ys) % ys == at % ys) & ((core - dc + cs) % cs == at // ys)
                picked = jnp.where(mine, piece.astype(F32), picked)
            total.append(picked)
        return jnp.concatenate(total, axis=1)

    grad_f = reduce_packet(keep_f, send_f)
    halves = [grad_f[:, i * packet : (i + 1) * packet] for i in range(2)]
    grad_project = jnp.concatenate([h[:, :ph] for h in halves], axis=1)
    grad_widen = jnp.concatenate([h[:, ph : ph + wh] for h in halves], axis=1)
    grad_narrow = jnp.concatenate(
        [
            jnp.concatenate(
                [h[:, ph + wh + j * ph : ph + wh + (j + 1) * ph] for h in halves], axis=1
            )
            for j in range(per)
        ],
        axis=0,
    )
    grad_attend = reduce_packet(keep_a, send_a)

    dp = jnp.transpose(dpool[:, :nshard], (1, 0, 2)).reshape(xs, zs, seq_count, width)
    level = add([send(dp[:, k], dz=-k) if k else dp[:, 0] for k in range(zs)], BF)
    own = add([send(level[k], dx=-k) if k else level[0] for k in range(xs)], F32)
    seqs = 4
    tokens_grad = pl.pallas_call(
        functools.partial(last_kernel, seqs=seqs, span=span),
        grid=(seq_count // seqs,),
        in_specs=[
            smem,
            pl.BlockSpec((seqs * span, width), lambda i: (i, 0)),
            pl.BlockSpec((seqs * span, width), lambda i: (i, 0)),
            pl.BlockSpec((seqs, 1, width), lambda i: (i, 0, 0)),
            pl.BlockSpec((1, width), lambda i: (0, 0)),
        ],
        out_specs=pl.BlockSpec((seqs * span, width), lambda i: (i, 0)),
        out_shape=jax.ShapeDtypeStruct((rows, width), F32),
        compiler_params=params(24),
        name="last",
    )(rel, part, x2, own.reshape(seq_count, 1, width), gain1)

    vec = jnp.concatenate(
        [vec_f[0].reshape(nshard, hs)]
        + [
            v.reshape(nshard, rps)
            for v in (vec_f[1, :width], vec_a[0], vec_a[1], vec_f[2, :width], vec_f[3, :width])
        ],
        axis=1,
    )
    quarter = -(-vec.shape[1] // (ys * cs * 128)) * 128
    vec = jnp.pad(vec, ((0, 0), (0, quarter * ys * cs - vec.shape[1])))
    half = quarter * ys
    vec = reduce_packet(
        lax.dynamic_slice_in_dim(vec, core * half, half, 1),
        lax.dynamic_slice_in_dim(vec, (1 - core) * half, half, 1),
    )[0]
    vecs = [vec[:hs]] + [vec[hs + i * rps : hs + (i + 1) * rps] for i in range(5)]
    return (
        block_out.reshape(tokens.shape),
        tokens_grad.reshape(tokens.shape),
        grad_attend,
        grad_project,
        grad_widen,
        grad_narrow,
        *vecs,
    )


def solution(mesh):
    first = mesh.devices[0]
    xs = len({d.coords[0] for d in first})
    cs = len({d.core_on_chip for d in mesh.devices[:, 0]})
    sizes = (mesh.shape["shard"] // xs, xs, mesh.shape["rep"] // cs, cs)
    row = P("shard", None)
    vec = P("shard")
    act = P("rep", "shard", None)
    return jax.shard_map(
        functools.partial(local, sizes=sizes),
        mesh=mesh,
        in_specs=(act, act, P("rep", None), row, row, row, row) + (vec,) * 6,
        out_specs=(act, act, row, row, row, row) + (vec,) * 6,
        check_vma=False,
    )
```

```python
import functools

import jax
import jax.numpy as jnp
from jax import lax
from jax.experimental import pallas as pl
from jax.experimental.pallas import tpu as pltpu
from jax.sharding import PartitionSpec as P

HEADS = 8
epsilon = 1e-05
masked = -1e30
F32 = jnp.float32
BF = jnp.bfloat16
MIB = 1 << 20


def dot(a, b):
    return jnp.dot(a, b, preferred_element_type=F32)


def dot_nt(a, b):
    return lax.dot_general(a, b, (((1,), (1,)), ((), ())), preferred_element_type=F32)


def dot_tn(a, b):
    return lax.dot_general(a, b, (((0,), (0,)), ((), ())), preferred_element_type=F32)


def normed(v):
    center = v - jnp.mean(v, axis=-1, keepdims=True)
    rstd = lax.rsqrt(jnp.mean(center * center, axis=-1, keepdims=True) + epsilon)
    return center * rstd, rstd


def norm_back(e, n, rstd):
    return rstd * (
        e - jnp.mean(e, axis=-1, keepdims=True) - n * jnp.mean(e * n, axis=-1, keepdims=True)
    )


def two_heads_lanes(t):
    half = t.shape[0] // 2
    zero = jnp.zeros((half, t.shape[1]), t.dtype)
    left = jnp.concatenate([t[:half], zero], axis=0)
    right = jnp.concatenate([zero, t[half:]], axis=0)
    return jnp.concatenate([left, right], axis=1)


def two_heads_rows(a):
    first = lax.broadcasted_iota(jnp.int32, a.shape, 1) < a.shape[1] // 2
    zero = jnp.zeros_like(a)
    return jnp.concatenate([jnp.where(first, a, zero), jnp.where(first, zero, a)], axis=0)


def diagonal(t):
    rows, cols = t.shape[0] // 2, t.shape[1] // 2
    return jnp.concatenate([t[:rows, :cols], t[rows:, cols:]], axis=0)


def span_bias(doc_from, pooled):
    span = doc_from.shape[1]
    key = lax.broadcasted_iota(jnp.int32, (span, span), 0)
    query = lax.broadcasted_iota(jnp.int32, (span, span), 1)
    direct = jnp.where((key >= doc_from) & (key <= query), 0.0, masked).astype(F32)
    both = jnp.concatenate([direct, pooled], axis=0)
    return jnp.concatenate([both, both], axis=1)


def arriving(meta, sizes, pieces, places, sems, act, kind):
    zs, xs = sizes
    z, x, core = meta[0], meta[1], meta[2]
    at = 0
    for which in range(2):
        half = core if which == 0 else 1 - core
        for kx in range(xs):
            for kz in range(zs):
                shard = lax.rem(z - kz + zs, zs) * xs + lax.rem(x - kx + xs, xs)
                for src, dst in places[kind](pieces, which, kx, kz, shard, half):
                    copy = pltpu.make_async_copy(src, dst, sems.at[kind, at])
                    copy.start() if act == "start" else copy.wait()
                    at += 1


def pool_kernel(rel_ref, x_ref, out_ref, *, seqs, span):
    n, _ = normed(x_ref[...].astype(F32))
    for i in range(seqs):
        first = rel_ref[pl.program_id(0) * seqs + i]
        row = lax.broadcasted_iota(jnp.int32, (span, n.shape[1]), 0)
        part = jnp.where(row >= first, n[i * span : (i + 1) * span], 0.0)
        count = jnp.full((1, 1), span - first, jnp.int32).astype(F32)
        out_ref[i] = jnp.sum(part, axis=0, keepdims=True) / count


def padded(a, rows, value):
    shape = a.shape[:-2] + (rows - a.shape[-2], a.shape[-1])
    return jnp.concatenate([a, jnp.full(shape, value, a.dtype)], axis=-2) if shape[-2] else a


def vector(vecs_ref, i):
    return vecs_ref[i : i + 1, :]


def attend_kernel(meta, *refs, sizes, seqs, span, rps, whole):
    x_ref, vecs_ref, pool_ref, from_ref, pbias_ref = refs[:5]
    width = x_ref.shape[1]
    first = pl.program_id(0) == 0
    if whole:
        w_ref, _, _, _, qkv_ref, o_ref, lse_ref = refs[5:]
    else:
        xs = sizes[1]
        pieces = refs[5 : 5 + 2 * xs]
        w_ref, qkv_ref, o_ref, lse_ref, sems = refs[5 + 2 * xs :]
        nh = w_ref.shape[1] // 2

        def place(pieces, which, kx, kz, shard, half):
            yield (
                pieces[which * xs + kx].at[pl.ds(kz * rps, rps), :],
                w_ref.at[
                    pl.ds(pl.multiple_of(shard * rps, rps), rps),
                    pl.ds(pl.multiple_of(half * nh, 128), nh),
                ],
            )

        @pl.when(first)
        def _():
            arriving(meta, sizes, pieces, [place], sems, "start", 0)

    gain, shift = vector(vecs_ref, 1), vector(vecs_ref, 2)
    n, _ = normed(x_ref[...].astype(F32))
    h = (n * gain + shift).astype(BF)
    cp = -(-pool_ref.shape[1] // 16) * 16
    pooled_h = padded(pool_ref[...], cp, 0.0).reshape(seqs * cp, width) * gain + shift
    if not whole:

        @pl.when(first)
        def _():
            arriving(meta, sizes, pieces, [place], sems, "wait", 0)

    qkv = dot(h, w_ref[...]).astype(BF)
    q = qkv[:, :width] * jnp.asarray((width // HEADS) ** -0.5, BF)
    qkv_ref[:, :width] = q
    qkv_ref[:, width:] = qkv[:, width:]
    kvb = dot(pooled_h.astype(BF), w_ref[:, width:]).astype(BF)
    pairs = range(HEADS // 2)
    col = lambda part, p: slice(part * width + p * 128, part * width + (p + 1) * 128)
    for s in range(seqs):
        rows = slice(s * span, (s + 1) * span)
        prow = slice(s * cp, (s + 1) * cp)
        bias = span_bias(from_ref[s], padded(pbias_ref[s], cp, masked))
        both = lambda part, p: jnp.concatenate(
            [qkv[rows, col(part, p)], kvb[prow, col(part - 1, p)]], axis=0
        )
        query = [two_heads_lanes(q[rows, col(0, p)].T) for p in pairs]
        scores = [dot(both(1, p), query[p]) + bias for p in pairs]
        top = [jnp.max(scores[p], axis=0, keepdims=True) for p in pairs]
        e = [jnp.exp(scores[p] - top[p]) for p in pairs]
        total = [jnp.sum(e[p], axis=0, keepdims=True) for p in pairs]
        prob = [(e[p] * (1.0 / total[p])).astype(BF) for p in pairs]
        out = [diagonal(dot_tn(both(2, p), prob[p])).astype(BF) for p in pairs]
        for p in pairs:
            lse_ref[s, p : p + 1, :] = top[p] + jnp.log(total[p])
            o_ref[rows, col(0, p)] = out[p].T


def ffn_kernel(meta, *refs, sizes, rps):
    o_ref, x_ref, y_ref, vecs_ref = refs[:4]
    pieces = refs[4:8]
    (
        dr_ref,
        a_ref,
        keep_ref,
        send_ref,
        wp_ref,
        w2_ref,
        vec_ref,
        w1_ref,
        acc1_ref,
        acc2_ref,
        accp_ref,
        sems,
    ) = refs[8:]
    width, hidden = w1_ref.shape
    zs = sizes[0]
    per = hidden // width
    ph, wh = width // 2, hidden // 2
    step = pl.program_id(0)

    def source(ref, kx, kz):
        return ref, pl.ds((kx * zs + kz) * rps, rps)

    def place_p(pieces, which, kx, kz, shard, half):
        ref, src = source(pieces[which], kx, kz)
        yield (
            ref.at[src, pl.ds(0, ph)],
            wp_ref.at[
                pl.ds(pl.multiple_of(shard * rps, rps), rps),
                pl.ds(pl.multiple_of(half * ph, 128), ph),
            ],
        )

    def place_1(pieces, which, kx, kz, shard, half):
        ref, src = source(pieces[which], kx, kz)
        yield (
            ref.at[src, pl.ds(ph, wh)],
            w1_ref.at[
                pl.ds(pl.multiple_of(shard * rps, rps), rps),
                pl.ds(pl.multiple_of(half * wh, 128), wh),
            ],
        )

    def place_2(pieces, which, kx, kz, shard, half):
        ref, src = source(pieces[2 + which], kx, kz)
        for j in range(per // 2):
            at = (shard * per + half * (per // 2) + j) * rps
            yield (
                ref.at[src, pl.ds(j * width, width)],
                w2_ref.at[pl.ds(pl.multiple_of(at, rps), rps), :],
            )

    def weights(act, kind):
        @pl.when(step == 0)
        def _():
            arriving(meta, sizes, pieces, [place_p, place_1, place_2], sems, act, kind)

    for kind in range(3):
        weights("start", kind)

    @pl.when(step == 0)
    def _():
        acc1_ref[...] = jnp.zeros_like(acc1_ref)
        acc2_ref[...] = jnp.zeros_like(acc2_ref)
        accp_ref[...] = jnp.zeros_like(accp_ref)
        vec_ref[...] = jnp.zeros_like(vec_ref)

    weights("wait", 0)
    o, y = o_ref[...], y_ref[...]
    r1 = x_ref[...].astype(F32) + dot(o, wp_ref[...])
    n, rstd = normed(r1)
    gain = vector(vecs_ref, 3)
    h = (n * gain + vector(vecs_ref, 4)).astype(BF)
    ht = h.T
    dh = jnp.zeros_like(r1)
    weights("wait", 1)
    weights("wait", 2)
    for j in range(per):
        at = slice(j * width, (j + 1) * width)
        u = dot(h, w1_ref[:, at]) + vecs_ref[5 + j : 6 + j, :]
        da = dot_nt(y, w2_ref[at, :])
        cdf = 0.5 + 0.5 * lax.erf(u * 0.7071067811865476)
        pdf = jnp.exp(u * u * -0.5) * 0.3989422804014327
        a = (u * cdf).astype(BF)
        du = (da * (cdf + u * pdf)).astype(BF)
        a_ref[:, at] = a
        dh += dot_nt(du, w1_ref[:, at])
        acc1_ref[:, at] += dot(ht, du)
        acc2_ref[at, :] += dot_tn(a, y)
        vec_ref[0:1, at] += jnp.sum(du.astype(F32), axis=0, keepdims=True)
    yf = y.astype(F32)
    dr = yf + norm_back(dh * gain, n, rstd)
    dr_ref[...] = dr
    accp_ref[...] += dot_tn(o, dr.astype(BF))
    vec_ref[1:2, :width] += jnp.sum(yf, axis=0, keepdims=True)
    vec_ref[2:3, :width] += jnp.sum(dh * n, axis=0, keepdims=True)
    vec_ref[3:4, :width] += jnp.sum(dh, axis=0, keepdims=True)

    @pl.when(step == pl.num_programs(0) - 1)
    def _():
        for which, ref in ((0, keep_ref), (1, send_ref)):
            half = meta[2] if which == 0 else 1 - meta[2]
            pcol = pl.ds(pl.multiple_of(half * ph, 128), ph)
            ref[:, :ph] = accp_ref[:, pcol].astype(BF)
            ref[:, ph : ph + wh] = acc1_ref[:, pl.ds(pl.multiple_of(half * wh, 128), wh)].astype(BF)
            for shard in range(width // rps):
                for j in range(per):
                    at = (shard * per + j) * rps
                    ref[shard * rps : (shard + 1) * rps, ph + wh + j * ph : ph + wh + (j + 1) * ph] = (
                        acc2_ref[at : at + rps, pcol].astype(BF)
                    )


def out_kernel(o_ref, x_ref, a_ref, vecs_ref, wp_ref, w2_ref, out_ref):
    r1 = x_ref[...].astype(F32) + dot(o_ref[...], wp_ref[...])
    out_ref[...] = r1 + dot(a_ref[...], w2_ref[...]) + vector(vecs_ref, 0)


def back_kernel(meta, *refs, seqs, span, begin):
    (
        dr_ref,
        x_ref,
        qkv_ref,
        lse_ref,
        w_ref,
        wp_ref,
        vecs_ref,
        pool_ref,
        from_ref,
        pbias_ref,
    ) = refs[:10]
    if begin:
        dqkv_ref, dpool_ref, acc_ref, dkvb_ref = refs[10:]
    else:
        sum_ref, _, _, dqkv_ref, dpool_ref, keep_ref, send_ref, vec_ref, acc_ref, dkvb_ref = refs[10:]
    width = x_ref.shape[1]
    scale = (width // HEADS) ** -0.5
    step = pl.program_id(0)

    @pl.when(step == 0)
    def _():
        acc_ref[...] = jnp.zeros_like(acc_ref) if begin else sum_ref[...]

    gain, shift = vector(vecs_ref, 1), vector(vecs_ref, 2)
    cp = -(-pool_ref.shape[1] // 16) * 16
    pool = padded(pool_ref[...], cp, 0.0).reshape(seqs * cp, width)
    pooled_h = (pool * gain + shift).astype(BF)
    kvb = dot(pooled_h, w_ref[:, width:]).astype(BF)
    dr = dr_ref[...]
    do = dot_nt(dr.astype(BF), wp_ref[...]).astype(BF)
    pairs = range(HEADS // 2)
    col = lambda part, p: slice(part * width + p * 128, part * width + (p + 1) * 128)
    for s in range(seqs):
        rows = slice(s * span, (s + 1) * span)
        prow = slice(s * cp, (s + 1) * cp)
        bias = span_bias(from_ref[s], padded(pbias_ref[s], cp, masked))
        both = lambda part, p: jnp.concatenate(
            [qkv_ref[rows, col(part, p)], kvb[prow, col(part - 1, p)]], axis=0
        )
        q = [qkv_ref[rows, col(0, p)] for p in pairs]
        g = [do[rows, col(0, p)] for p in pairs]
        keys = [both(1, p) for p in pairs]
        scores = [dot(keys[p], two_heads_lanes(q[p].T)) + bias for p in pairs]
        dprob = [dot(both(2, p), two_heads_lanes(g[p].T)) for p in pairs]
        prob = [jnp.exp(scores[p] - lse_ref[s, p : p + 1, :]) for p in pairs]
        weighted = [prob[p] * dprob[p] for p in pairs]
        ds = [
            (weighted[p] - prob[p] * jnp.sum(weighted[p], axis=0, keepdims=True)).astype(BF)
            for p in pairs
        ]
        dv = [dot(prob[p].astype(BF), two_heads_rows(g[p])).astype(BF) for p in pairs]
        dq = [(diagonal(dot_tn(keys[p], ds[p])) * scale).astype(BF) for p in pairs]
        dk = [dot(ds[p], two_heads_rows(q[p])).astype(BF) for p in pairs]
        for p in pairs:
            dqkv_ref[rows, col(0, p)] = dq[p].T
            dqkv_ref[rows, col(1, p)] = dk[p][:span]
            dqkv_ref[rows, col(2, p)] = dv[p][:span]
            dkvb_ref[prow, col(0, p)] = dk[p][span:]
            dkvb_ref[prow, col(1, p)] = dv[p][span:]
    n, _ = normed(x_ref[...].astype(F32))
    h = (n * gain + shift).astype(BF)
    dqkv, dkvb = dqkv_ref[...], dkvb_ref[...]
    acc_ref[:width] += dot_tn(h, dqkv)
    acc_ref[:width, width:] += dot_tn(pooled_h, dkvb)
    acc_ref[width : width + 1] += jnp.sum(dqkv.astype(F32), axis=0, keepdims=True)
    acc_ref[width : width + 1, width:] += jnp.sum(dkvb.astype(F32), axis=0, keepdims=True)
    dpool_ref[...] = dot_nt(dkvb, w_ref[:, width:]).astype(BF).reshape(seqs, cp, width)
    if begin:
        return

    @pl.when(step == pl.num_programs(0) - 1)
    def _():
        nh = acc_ref.shape[1] // 2
        for which, ref in ((0, keep_ref), (1, send_ref)):
            half = meta[2] if which == 0 else 1 - meta[2]
            ref[...] = acc_ref[:width, pl.ds(pl.multiple_of(half * nh, 128), nh)].astype(BF)
        w = w_ref[...].astype(F32)

        def row(m):
            total = jnp.sum(m, axis=1, keepdims=True)
            return jnp.broadcast_to(total, (width, 128)).T[:1]

        dshift = row(w * acc_ref[width : width + 1])
        dgain = (row(w * acc_ref[:width]) - shift * dshift) / gain
        vec_ref[0:1] = dgain
        vec_ref[1:2] = dshift


def last_kernel(rel_ref, dr_ref, x_ref, dqkv_ref, w_ref, dpool_ref, vecs_ref, out_ref, *, seqs, span):
    n, rstd = normed(x_ref[...].astype(F32))
    dh = dot_nt(dqkv_ref[...], w_ref[...])
    for i in range(seqs):
        first = rel_ref[pl.program_id(0) * seqs + i]
        rows = slice(i * span, (i + 1) * span)
        count = jnp.full((1, 1), span - first, jnp.int32).astype(F32)
        share = dpool_ref[i] / count
        row = lax.broadcasted_iota(jnp.int32, (span, n.shape[1]), 0)
        e = (dh[rows] + jnp.where(row >= first, share, 0.0)) * vector(vecs_ref, 1)
        out_ref[rows, :] = dr_ref[rows, :] + norm_back(e, n[rows], rstd[rows])


def after(a, *first):
    return lax.optimization_barrier((a, *first))[0]


def params(mib):
    return pltpu.CompilerParams(dimension_semantics=("arbitrary",), vmem_limit_bytes=mib * MIB)


LITTLE = pl.CostEstimate(flops=1, bytes_accessed=1, transcendentals=0)


def local(
    tokens,
    cotangent,
    doc_lengths,
    attend,
    project,
    widen,
    narrow,
    hidden_bias,
    final_bias,
    gain_first,
    shift_first,
    gain_second,
    shift_second,
    *,
    sizes,
):
    zs, xs, ys, cs = sizes
    nshard = zs * xs
    seq_count, span, width = tokens.shape
    rows = seq_count * span
    hidden = widen.shape[1]
    rps = attend.shape[0]
    rep, shard = lax.axis_index("rep"), lax.axis_index("shard")
    z, x, y, core = shard // xs, shard % xs, rep // cs, rep % cs
    meta = jnp.stack([z, x, core]).astype(jnp.int32)

    def send(a, dz=0, dx=0, dy=0, dc=0):
        perm = []
        for r in range(ys * cs):
            for s in range(nshard):
                r2 = (r // cs + dy) % ys * cs + (r % cs + dc) % cs
                s2 = (s // xs + dz) % zs * xs + (s % xs + dx) % xs
                perm.append((r * nshard + s, r2 * nshard + s2))
        return lax.ppermute(a, ("rep", "shard"), perm)

    def levels(a):
        return jnp.concatenate([a] + [send(a, dz=k) for k in range(1, zs)], axis=0)

    def sides(a):
        return [a] + [send(a, dx=k) for k in range(1, xs)]

    ndoc = doc_lengths.shape[1]
    upto = jnp.arange(ndoc)[:, None] <= jnp.arange(ndoc)[None, :]
    ends = jnp.sum(jnp.where(upto[None], doc_lengths[:, :, None], 0), axis=1, dtype=jnp.int32)
    starts = ends - doc_lengths
    base = shard * span
    positions = base + jnp.arange(span, dtype=jnp.int32)
    segment = jnp.sum(
        (positions[None, :, None] >= ends[:, None, :]).astype(jnp.int32), axis=-1, dtype=jnp.int32
    )

    def start_at(at):
        before = starts[:, None, :] <= at[..., None]
        return jnp.max(jnp.where(before, starts[:, None, :], 0), axis=-1)

    doc_from = (start_at(positions[None, :]) - base)[:, None, :]
    slot = jnp.arange(nshard, dtype=jnp.int32)
    slot_span = (z - slot % zs + zs) % zs * xs + (x - slot // zs + xs) % xs
    slot_last = slot_span * span + span - 1
    last_doc = jnp.sum(
        (slot_last[None, :, None] >= ends[:, None, :]).astype(jnp.int32), axis=-1, dtype=jnp.int32
    )
    counts = jnp.minimum(span, slot_last[None, :] + 1 - start_at(slot_last[None, :]))
    seen = (slot_span[None, :, None] < shard) & (last_doc[:, :, None] == segment[:, None, :])
    pbias = jnp.where(seen, jnp.log(counts.astype(F32))[:, :, None], masked)
    cp = max(16, -(-nshard // 16) * 16)
    rel = span - counts[:, 0]

    x2 = tokens.reshape(rows, width)
    y2 = cotangent.reshape(rows, width)
    smem = pl.BlockSpec(memory_space=pltpu.SMEM)
    hbm = pl.BlockSpec(memory_space=pl.ANY)
    nh = attend.shape[1] // 2
    attend_col = levels(lax.dynamic_slice_in_dim(attend, core * nh, nh, 1))
    pool_seqs = 4
    pool = pl.pallas_call(
        functools.partial(pool_kernel, seqs=pool_seqs, span=span),
        grid=(seq_count // pool_seqs,),
        in_specs=[smem, pl.BlockSpec((pool_seqs * span, width), lambda i: (i, 0))],
        out_specs=pl.BlockSpec((pool_seqs, 1, width), lambda i: (i, 0, 0)),
        out_shape=jax.ShapeDtypeStruct((seq_count, 1, width), F32),
        compiler_params=params(16),
        cost_estimate=LITTLE,
        name="pool",
    )(rel, after(x2, attend_col))
    per = hidden // width
    hs = hidden_bias.shape[0]

    def own_lanes(v):
        n = v.shape[1]
        at = jnp.arange(nshard * n, dtype=jnp.int32) // n
        return jnp.where(at == shard, jnp.tile(v.astype(F32), (1, nshard)), 0.0)

    small = jnp.stack([final_bias, gain_first, shift_first, gain_second, shift_second])
    packed = jnp.concatenate(
        [
            pool.reshape(seq_count, width),
            own_lanes(small),
            own_lanes(hidden_bias[None]).reshape(per, width),
        ],
        axis=0,
    )
    small_col = levels(packed)

    ph, wh = width // 2, hidden // 2
    half_p = jnp.concatenate(
        [
            lax.dynamic_slice_in_dim(project, core * ph, ph, 1),
            lax.dynamic_slice_in_dim(widen, core * wh, wh, 1),
        ],
        axis=1,
    )
    nhalf = lax.dynamic_slice_in_dim(narrow, core * (narrow.shape[0] // 2), narrow.shape[0] // 2, 0)
    half_n = jnp.concatenate([nhalf[j * rps : (j + 1) * rps] for j in range(per // 2)], axis=1)
    attend_cols = sides(attend_col)
    attend_parts = attend_cols + [send(m, dc=1) for m in attend_cols]
    widen_col = levels(after(half_p, attend_col, pool))
    small_cols = sides(small_col)
    narrow_col = levels(after(half_n, widen_col))
    widen_sides = sides(after(widen_col, *attend_parts, *small_cols))

    slots = jnp.concatenate(small_cols, axis=0).reshape(nshard, -1, width)
    pool_all = jnp.transpose(slots[:, :seq_count], (1, 0, 2))
    vectors = jnp.sum(slots[:, seq_count:], axis=0)
    nvectors = vectors.shape[0]

    seqs = 4
    calls = 2
    steps = seq_count // seqs // calls
    all_spec = lambda a, b: pl.BlockSpec((a, b), lambda i, m: (0, 0))
    row_spec = lambda n, w, c=0: pl.BlockSpec((n, w), lambda i, m: (i + c * steps, 0))
    seq_spec = lambda n, a, b, c=0: pl.BlockSpec((n, a, b), lambda i, m: (i + c * steps, 0, 0))
    act_specs = lambda c: [
        row_spec(seqs * span, 3 * width, c),
        row_spec(seqs * span, width, c),
        seq_spec(seqs, HEADS // 2, 2 * span, c),
    ]
    act_shapes = [
        jax.ShapeDtypeStruct((rows, 3 * width), BF),
        jax.ShapeDtypeStruct((rows, width), BF),
        jax.ShapeDtypeStruct((seq_count, HEADS // 2, 2 * span), F32),
    ]

    def attention(c, x2, weights, before):
        body = functools.partial(
            attend_kernel, sizes=(zs, xs), seqs=seqs, span=span, rps=rps, whole=c > 0
        )
        return pl.pallas_call(
            body,
            grid_spec=pltpu.PrefetchScalarGridSpec(
                num_scalar_prefetch=1,
                grid=(steps,),
                in_specs=[
                    row_spec(seqs * span, width, c),
                    all_spec(nvectors, width),
                    seq_spec(seqs, nshard, width, c),
                    seq_spec(seqs, 1, span, c),
                    seq_spec(seqs, nshard, span, c),
                ]
                + ([all_spec(width, 3 * width)] if c else [hbm] * len(weights))
                + [hbm] * len(before),
                out_specs=([] if c else [all_spec(width, 3 * width)]) + act_specs(c),
                scratch_shapes=[] if c else [pltpu.SemaphoreType.DMA((1, 2 * nshard))],
            ),
            out_shape=([] if c else [jax.ShapeDtypeStruct((width, 3 * width), BF)]) + act_shapes,
            input_output_aliases={7 + i: i for i in range(len(before))},
            compiler_params=params(58),
            cost_estimate=LITTLE,
            name="attention",
        )(meta, x2, vectors, pool_all, doc_from, pbias, *weights, *before)

    w_all, qkv, o, lse = attention(0, after(x2, widen_col), attend_parts, [])
    widen_mine = jnp.concatenate(after(widen_sides, lse), axis=0)
    narrow_sides = sides(after(narrow_col, lse))
    widen_other = send(widen_mine, dc=1)
    qkv, o, lse = attention(1, after(x2, narrow_col, widen_mine), [w_all], [qkv, o, lse])
    narrow_mine = jnp.concatenate(after(narrow_sides, lse), axis=0)
    ffn_parts = [widen_mine, widen_other, narrow_mine, send(narrow_mine, dc=1)]

    tile = 512
    packet = ph + wh + per * ph
    steps = 0
    dr, a, keep_f, send_f, wp_all, w2_all, vec_f = pl.pallas_call(
        functools.partial(ffn_kernel, sizes=(zs, xs), rps=rps),
        grid_spec=pltpu.PrefetchScalarGridSpec(
            num_scalar_prefetch=1,
            grid=(rows // tile,),
            in_specs=[
                row_spec(tile, width),
                row_spec(tile, width),
                row_spec(tile, width),
                all_spec(nvectors, width),
            ]
            + [hbm] * 4,
            out_specs=[
                row_spec(tile, width),
                row_spec(tile, hidden),
                all_spec(width, packet),
                all_spec(width, packet),
                all_spec(width, width),
                all_spec(hidden, width),
                all_spec(8, hidden),
            ],
            scratch_shapes=[
                pltpu.VMEM((width, hidden), BF),
                pltpu.VMEM((width, hidden), F32),
                pltpu.VMEM((hidden, width), F32),
                pltpu.VMEM((width, width), F32),
                pltpu.SemaphoreType.DMA((3, nshard * per)),
            ],
        ),
        out_shape=[
            jax.ShapeDtypeStruct((rows, width), F32),
            jax.ShapeDtypeStruct((rows, hidden), BF),
            jax.ShapeDtypeStruct((width, packet), BF),
            jax.ShapeDtypeStruct((width, packet), BF),
            jax.ShapeDtypeStruct((width, width), BF),
            jax.ShapeDtypeStruct((hidden, width), BF),
            jax.ShapeDtypeStruct((8, hidden), F32),
        ],
        compiler_params=params(58),
        cost_estimate=LITTLE,
        name="ffn",
    )(meta, o, x2, y2, vectors, *ffn_parts)

    def add(parts, kind):
        total = parts[0].astype(F32)
        for p in parts[1:]:
            total = total + p.astype(F32)
        return total.astype(kind)

    def over_x(a):
        piece = lambda dx: lax.dynamic_slice_in_dim(a, (x + dx) % xs, 1, 1)
        return add([send(piece(dx), dx=dx) if dx else piece(0) for dx in range(xs)], BF)

    def over_y(a):
        n = a.shape[-1] // ys
        piece = lambda dy: lax.dynamic_slice_in_dim(a, (y + dy) % ys * n, n, a.ndim - 1)
        return add([send(piece(dy), dy=dy) if dy else piece(0) for dy in range(ys)], BF)

    def over_z(a, cover):
        k = a.shape[0] // zs
        piece = lambda dz: lax.dynamic_slice_in_dim(a, (z + dz) % zs * k, k, 0)
        parts = [send(piece(dz), dz=dz) if dz else piece(0) for dz in range(zs)]
        return add(after(parts, cover), BF)

    def over_xy(part, cover):
        n = part.shape[1] // ys
        k = part.shape[0] // nshard
        view = part.reshape(zs, xs, k, ys * n)

        def corner(dx, dy):
            at = (0, (x + dx) % xs, 0, (y + dy) % ys * n)
            return lax.dynamic_slice(view, at, (zs, 1, k, n)).reshape(zs * k, n)

        parts = [
            send(corner(dx, dy), dx=dx, dy=dy) if dx or dy else corner(0, 0)
            for dx in range(xs)
            for dy in range(ys)
        ]
        return add(after(parts, cover), BF)

    def replicas(part):
        found = {
            (dy, dc): send(part, dy=dy, dc=dc) if dy or dc else part
            for dy in range(ys)
            for dc in range(cs)
        }
        total = []
        for at in range(ys * cs):
            picked = jnp.zeros(part.shape, F32)
            for (dy, dc), piece in found.items():
                mine = ((y - dy + ys) % ys == at % ys) & ((core - dc + cs) % cs == at // ys)
                picked = jnp.where(mine, piece.astype(F32), picked)
            total.append(picked)
        return total

    steps = seq_count // seqs // calls

    def back(c, dr, before):
        nacc = width + 8
        sums = [all_spec(nacc, 3 * width)]
        halves = [all_spec(width, 3 * width // 2)] * 2 + [all_spec(8, width)]
        half_shapes = [
            jax.ShapeDtypeStruct((width, 3 * width // 2), BF),
            jax.ShapeDtypeStruct((width, 3 * width // 2), BF),
            jax.ShapeDtypeStruct((8, width), F32),
        ]
        return pl.pallas_call(
            functools.partial(back_kernel, seqs=seqs, span=span, begin=c == 0),
            grid_spec=pltpu.PrefetchScalarGridSpec(
                num_scalar_prefetch=1,
                grid=(steps,),
                in_specs=[
                    row_spec(seqs * span, width, c),
                    row_spec(seqs * span, width, c),
                    row_spec(seqs * span, 3 * width, c),
                    seq_spec(seqs, HEADS // 2, 2 * span, c),
                    all_spec(width, 3 * width),
                    all_spec(width, width),
                    all_spec(nvectors, width),
                    seq_spec(seqs, nshard, width, c),
                    seq_spec(seqs, 1, span, c),
                    seq_spec(seqs, nshard, span, c),
                ]
                + ((sums + [hbm, hbm]) if c else []),
                out_specs=[row_spec(seqs * span, 3 * width, c), seq_spec(seqs, cp, width, c)]
                + (halves if c else sums),
                scratch_shapes=([pltpu.VMEM((nacc, 3 * width), F32)] if c else [])
                + [pltpu.VMEM((seqs * cp, 2 * width), BF)],
            ),
            out_shape=[
                jax.ShapeDtypeStruct((rows, 3 * width), BF),
                jax.ShapeDtypeStruct((seq_count, cp, width), BF),
            ]
            + (half_shapes if c else [jax.ShapeDtypeStruct((nacc, 3 * width), F32)]),
            input_output_aliases={12: 0, 13: 1} if c else {},
            compiler_params=params(58),
            cost_estimate=LITTLE,
            name="back",
        )(meta, dr, x2, qkv, lse, w_all, wp_all, vectors, pool_all, doc_from, pbias, *before)

    dqkv, dpool, sums = back(0, dr, [])
    part_f = add([keep_f, after(send(send_f, dc=1), sums)], BF)
    dqkv, dpool, keep_a, send_a, vec_a = back(1, after(dr, part_f), [sums, dqkv, dpool])
    kf = part_f.shape[0] // nshard
    view = part_f.reshape(zs, xs, kf, packet)
    first_f = over_x(view[:, :, : kf // 2])
    second_f = over_y(view[:, :, kf // 2 :])

    dpool, keep_a = after((dpool, keep_a), first_f, second_f)
    part_a = add([keep_a, send(send_a, dc=1)], BF)
    part_f = jnp.concatenate([over_y(first_f), over_x(second_f)], axis=2)
    part_f = part_f.reshape(zs * kf, packet // ys)
    out_tile = 256
    block_out = pl.pallas_call(
        out_kernel,
        grid=(rows // out_tile,),
        in_specs=[
            pl.BlockSpec((out_tile, width), lambda i: (i, 0)),
            pl.BlockSpec((out_tile, width), lambda i: (i, 0)),
            pl.BlockSpec((out_tile, hidden), lambda i: (i, 0)),
            pl.BlockSpec((nvectors, width), lambda i: (0, 0)),
            pl.BlockSpec((width, width), lambda i: (0, 0)),
            pl.BlockSpec((hidden, width), lambda i: (0, 0)),
        ],
        out_specs=pl.BlockSpec((out_tile, width), lambda i: (i, 0)),
        out_shape=jax.ShapeDtypeStruct((rows, width), F32),
        compiler_params=params(58),
        cost_estimate=LITTLE,
        name="out",
    )(after(o, part_a, part_f), x2, a, vectors, wp_all, w2_all)
    share_a = over_xy(part_a, block_out)
    share_f = over_z(part_f, block_out)
    later_a = share_a
    grad_f = jnp.concatenate(replicas(share_f), axis=1)
    halves = [grad_f[:, i * packet : (i + 1) * packet] for i in range(2)]
    grad_project = jnp.concatenate([h[:, :ph] for h in halves], axis=1)
    grad_widen = jnp.concatenate([h[:, ph : ph + wh] for h in halves], axis=1)
    grad_narrow = jnp.concatenate(
        [
            jnp.concatenate(
                [h[:, ph + wh + j * ph : ph + wh + (j + 1) * ph] for h in halves], axis=1
            )
            for j in range(per)
        ],
        axis=0,
    )

    vec = jnp.concatenate(
        [vec_f[0].reshape(per, width), vec_f[1:2, :width], vec_a[:2], vec_f[2:4, :width]], axis=0
    ).astype(BF)
    nvec = vec.shape[0]
    dp = jnp.transpose(dpool[:, :nshard], (1, 0, 2)).reshape(xs, zs, seq_count, width)
    dp = jnp.concatenate([dp, jnp.broadcast_to(vec, (xs, zs, nvec, width))], axis=2)
    level = [send(dp[:, k], dz=-k) if k else dp[:, 0] for k in range(zs)]
    level = add(after(level, block_out), BF)
    own = add([send(level[k], dx=-k) if k else level[0] for k in range(xs)], F32)
    own_vec = jnp.concatenate(
        [lax.dynamic_slice(own[seq_count:].reshape(nvec * width), (shard * hs,), (hs,))]
        + [
            lax.dynamic_slice(own[seq_count + per + i], (shard * rps,), (rps,))
            for i in range(5)
        ]
    ).astype(BF)
    seqs = 2
    tokens_grad = pl.pallas_call(
        functools.partial(last_kernel, seqs=seqs, span=span),
        grid=(seq_count // seqs,),
        in_specs=[
            smem,
            pl.BlockSpec((seqs * span, width), lambda i: (i, 0)),
            pl.BlockSpec((seqs * span, width), lambda i: (i, 0)),
            pl.BlockSpec((seqs * span, 3 * width), lambda i: (i, 0)),
            pl.BlockSpec((width, 3 * width), lambda i: (0, 0)),
            pl.BlockSpec((seqs, 1, width), lambda i: (i, 0, 0)),
            pl.BlockSpec((nvectors, width), lambda i: (0, 0)),
        ],
        out_specs=pl.BlockSpec((seqs * span, width), lambda i: (i, 0)),
        out_shape=jax.ShapeDtypeStruct((rows, width), F32),
        compiler_params=params(58),
        cost_estimate=LITTLE,
        name="last",
    )(rel, after(dr, later_a), x2, dqkv, w_all, own[:seq_count].reshape(seq_count, 1, width), vectors)

    share_a = over_z(share_a, tokens_grad)
    ncol = share_a.shape[1]
    vrows = -(-own_vec.shape[0] // ncol)
    own_vec = jnp.pad(own_vec, (0, vrows * ncol - own_vec.shape[0])).reshape(vrows, ncol)
    found = replicas(jnp.concatenate([share_a, own_vec], axis=0))
    grad_attend = jnp.concatenate([f[:rps] for f in found], axis=1)
    vec = sum(f[rps:] for f in found).reshape(vrows * ncol)
    vecs = [vec[:hs]] + [vec[hs + i * rps : hs + (i + 1) * rps] for i in range(5)]
    return (
        block_out.reshape(tokens.shape),
        tokens_grad.reshape(tokens.shape),
        grad_attend,
        grad_project,
        grad_widen,
        grad_narrow,
        *vecs,
    )


def solution(mesh):
    first = mesh.devices[0]
    xs = len({d.coords[0] for d in first})
    cs = len({d.core_on_chip for d in mesh.devices[:, 0]})
    sizes = (mesh.shape["shard"] // xs, xs, mesh.shape["rep"] // cs, cs)
    row = P("shard", None)
    vec = P("shard")
    act = P("rep", "shard", None)
    return jax.shard_map(
        functools.partial(local, sizes=sizes),
        mesh=mesh,
        in_specs=(act, act, P("rep", None), row, row, row, row) + (vec,) * 6,
        out_specs=(act, act, row, row, row, row) + (vec,) * 6,
        check_vma=False,
    )
```

```python
import functools

import jax
import jax.numpy as jnp
from jax import lax
from jax.experimental import pallas as pl
from jax.experimental.pallas import tpu as pltpu
from jax.sharding import PartitionSpec as P

HEADS = 8
epsilon = 1e-05
masked = -1e30
F32 = jnp.float32
BF = jnp.bfloat16
MIB = 1 << 20


def dot(a, b):
    return jnp.dot(a, b, preferred_element_type=F32)


def dot_nt(a, b):
    return lax.dot_general(a, b, (((1,), (1,)), ((), ())), preferred_element_type=F32)


def dot_tn(a, b):
    return lax.dot_general(a, b, (((0,), (0,)), ((), ())), preferred_element_type=F32)


def normed(v):
    center = v - jnp.mean(v, axis=-1, keepdims=True)
    rstd = lax.rsqrt(jnp.mean(center * center, axis=-1, keepdims=True) + epsilon)
    return center * rstd, rstd


def norm_back(e, n, rstd):
    return rstd * (
        e - jnp.mean(e, axis=-1, keepdims=True) - n * jnp.mean(e * n, axis=-1, keepdims=True)
    )


def two_heads_lanes(t):
    half = t.shape[0] // 2
    zero = jnp.zeros((half, t.shape[1]), t.dtype)
    left = jnp.concatenate([t[:half], zero], axis=0)
    right = jnp.concatenate([zero, t[half:]], axis=0)
    return jnp.concatenate([left, right], axis=1)


def two_heads_rows(a):
    first = lax.broadcasted_iota(jnp.int32, a.shape, 1) < a.shape[1] // 2
    zero = jnp.zeros_like(a)
    return jnp.concatenate([jnp.where(first, a, zero), jnp.where(first, zero, a)], axis=0)


def diagonal(t):
    rows, cols = t.shape[0] // 2, t.shape[1] // 2
    return jnp.concatenate([t[:rows, :cols], t[rows:, cols:]], axis=0)


def span_bias(doc_from, pooled):
    span = doc_from.shape[1]
    key = lax.broadcasted_iota(jnp.int32, (span, span), 0)
    query = lax.broadcasted_iota(jnp.int32, (span, span), 1)
    direct = jnp.where((key >= doc_from) & (key <= query), 0.0, masked).astype(F32)
    both = jnp.concatenate([direct, pooled], axis=0)
    return jnp.concatenate([both, both], axis=1)


def arriving(meta, sizes, pieces, places, sems, act, kind):
    zs, xs = sizes
    z, x, core = meta[0], meta[1], meta[2]
    at = 0
    for which in range(2):
        half = core if which == 0 else 1 - core
        for kx in range(xs):
            for kz in range(zs):
                shard = (z ^ kz) * xs + (x ^ kx)
                for src, dst in places[kind](pieces, which, kx, kz, shard, half):
                    copy = pltpu.make_async_copy(src, dst, sems.at[kind, at])
                    copy.start() if act == "start" else copy.wait()
                    at += 1


def doc_starts(len_ref, seq):
    starts = [jnp.int32(0)]
    for j in range(len_ref.shape[1] - 1):
        starts.append(starts[-1] + len_ref[seq, j])
    return starts


def start_at(starts, position):
    found = jnp.zeros_like(position)
    for start in starts:
        found = jnp.where(position >= start, start, found)
    return found


def first_member(starts, base, span):
    return jnp.maximum(start_at(starts, base + span - 1) - base, 0)


def prep_kernel(meta, len_ref, x_ref, small_ref, hidden_ref, out_ref, from_ref, pbias_ref, *, sizes, seqs):
    zs, xs = sizes
    z, x = meta[0], meta[1]
    shard = z * xs + x
    nshard, span = pbias_ref.shape[1:]
    width = x_ref.shape[1]
    total = out_ref.shape[0] - small_ref.shape[0] - 4
    step = pl.program_id(0)
    base = shard * span

    @pl.when(step == 0)
    def _():
        def place(v, at):
            row = lax.broadcasted_iota(jnp.int32, (v.shape[1], width), 0)
            lane = lax.broadcasted_iota(jnp.int32, (v.shape[1], width), 1)
            return dot(v, (lane == row + at).astype(F32).astype(BF))

        nsmall, n = small_ref.shape
        rows = [place(small_ref[...], shard * n)]
        for r in range(4):
            rows.append(place(hidden_ref[...], shard * hidden_ref.shape[1] - r * width))
        out_ref[total:, :] = jnp.concatenate(rows, axis=0)

    n, _ = normed(x_ref[...].astype(F32))
    row = lax.broadcasted_iota(jnp.int32, (span, width), 0)
    slot = lax.broadcasted_iota(jnp.int32, (nshard, span), 0)
    slot_last = slot * span + span - 1
    position = base + lax.broadcasted_iota(jnp.int32, (1, span), 1)
    pooled = []
    for i in range(seqs):
        starts = doc_starts(len_ref, step * seqs + i)
        first = first_member(starts, base, span)
        part = jnp.where(row >= first, n[i * span : (i + 1) * span], 0.0)
        count = jnp.full((1, 1), span - first, jnp.int32).astype(F32)
        pooled.append(jnp.sum(part, axis=0, keepdims=True) / count)
        here = start_at(starts, position)
        from_ref[i] = here - base
        last = start_at(starts, slot_last)
        counts = jnp.minimum(span, slot_last + 1 - last).astype(F32)
        seen = (slot < shard) & (last == here)
        pbias_ref[i] = jnp.where(seen, jnp.log(counts), masked)
    at = pl.multiple_of(step * seqs, seqs)
    out_ref[pl.ds(at, seqs), :] = jnp.concatenate(pooled, axis=0)


def padded(a, rows, value):
    shape = a.shape[:-2] + (rows - a.shape[-2], a.shape[-1])
    return jnp.concatenate([a, jnp.full(shape, value, a.dtype)], axis=-2) if shape[-2] else a


def vector(slots_ref, i, nslot):
    total = slots_ref.shape[0] // nslot
    at = [k * total + total - 9 + i for k in range(nslot)]
    return sum(slots_ref[k : k + 1, :] for k in at)


def pooled_tokens(meta, slots_ref, seq, sizes, cp):
    zs, xs = sizes
    nslot = zs * xs
    total = slots_ref.shape[0] // nslot
    rows = []
    for span in range(nslot):
        slot = (meta[1] ^ (span % xs)) * zs + (meta[0] ^ (span // xs))
        rows.append(slots_ref[pl.ds(slot * total + seq, 1), :])
    return padded(jnp.concatenate(rows, axis=0), cp, 0.0)


def attend_kernel(meta, *refs, sizes, seqs, span, rps, start):
    x_ref, slots_ref, from_ref, pbias_ref = refs[:4]
    width = x_ref.shape[1]
    nslot = pbias_ref.shape[1]
    cp = -(-nslot // 16) * 16
    gain, shift = vector(slots_ref, 1, nslot), vector(slots_ref, 2, nslot)
    seq0 = pl.program_id(0) * seqs + start
    if start:
        w_ref, _, _, _, qkv_ref, o_ref, lse_ref = refs[4:]
    else:
        xs = sizes[1]
        pieces = refs[4 : 4 + 2 * xs]
        w_ref, qkv_ref, o_ref, lse_ref, sems = refs[4 + 2 * xs :]
        nh = w_ref.shape[1] // 2

        def place(pieces, which, kx, kz, shard, half):
            yield (
                pieces[which * xs + kx].at[pl.ds(kz * rps, rps), :],
                w_ref.at[
                    pl.ds(pl.multiple_of(shard * rps, rps), rps),
                    pl.ds(pl.multiple_of(half * nh, 128), nh),
                ],
            )

        @pl.when(pl.program_id(0) == 0)
        def _():
            arriving(meta, sizes, pieces, [place], sems, "start", 0)

    n, _ = normed(x_ref[...].astype(F32))
    h = (n * gain + shift).astype(BF)
    pooled_h = jnp.concatenate(
        [pooled_tokens(meta, slots_ref, seq0 + i, sizes, cp) for i in range(seqs)], axis=0
    )
    pooled_h = pooled_h * gain + shift
    if not start:

        @pl.when(pl.program_id(0) == 0)
        def _():
            arriving(meta, sizes, pieces, [place], sems, "wait", 0)

    qkv = dot(h, w_ref[...]).astype(BF)
    q = qkv[:, :width] * jnp.asarray((width // HEADS) ** -0.5, BF)
    qkv_ref[:, :width] = q
    qkv_ref[:, width:] = qkv[:, width:]
    kvb = dot(pooled_h.astype(BF), w_ref[:, width:]).astype(BF)
    pairs = range(HEADS // 2)
    col = lambda part, p: slice(part * width + p * 128, part * width + (p + 1) * 128)
    for s in range(seqs):
        rows = slice(s * span, (s + 1) * span)
        prow = slice(s * cp, (s + 1) * cp)
        bias = span_bias(from_ref[s], padded(pbias_ref[s], cp, masked))
        both = lambda part, p: jnp.concatenate(
            [qkv[rows, col(part, p)], kvb[prow, col(part - 1, p)]], axis=0
        )
        query = [two_heads_lanes(q[rows, col(0, p)].T) for p in pairs]
        scores = [dot(both(1, p), query[p]) + bias for p in pairs]
        top = [jnp.max(scores[p], axis=0, keepdims=True) for p in pairs]
        e = [jnp.exp(scores[p] - top[p]) for p in pairs]
        total = [jnp.sum(e[p], axis=0, keepdims=True) for p in pairs]
        prob = [(e[p] * (1.0 / total[p])).astype(BF) for p in pairs]
        out = [diagonal(dot_tn(both(2, p), prob[p])).astype(BF) for p in pairs]
        for p in pairs:
            lse_ref[s, p : p + 1, :] = top[p] + jnp.log(total[p])
            o_ref[rows, col(0, p)] = out[p].T


def ffn_kernel(meta, *refs, rps, places, nslot):
    o_ref, x_ref, y_ref, slots_ref = refs[:4]
    pieces = refs[4 : 4 + len(places)]
    (
        out_ref,
        dr_ref,
        keep_ref,
        send_ref,
        wp_ref,
        vec_ref,
        all_ref,
        w2_ref,
        acc1_ref,
        acc2_ref,
        accp_ref,
        sems,
    ) = refs[4 + len(places) :]
    hidden, width = w2_ref.shape
    per = hidden // width
    quarter = all_ref.shape[1] // 4
    pq = width // 4
    ph, wh = width // 2, hidden // 2
    step = pl.program_id(0)

    def weights(act):
        z, x, core, pair = meta[0], meta[1], meta[2], meta[3]
        xs = meta[4]
        at = 0
        for ref, place in zip(pieces, places):
            for row, rows, kz, kx, ky, kc, part in place:
                shard = (z ^ kz) * xs + (x ^ kx)
                col = ((pair ^ ky) * 2 + (core ^ kc)) * quarter
                copy = pltpu.make_async_copy(
                    ref.at[pl.ds(row, rows), :],
                    all_ref.at[
                        pl.ds(pl.multiple_of(shard * rps + part, rows), rows),
                        pl.ds(pl.multiple_of(col, 128), quarter),
                    ],
                    sems.at[at],
                )
                copy.start() if act == "start" else copy.wait()
                at += 1

    @pl.when(step == 0)
    def _():
        weights("start")
        acc1_ref[...] = jnp.zeros_like(acc1_ref)
        acc2_ref[...] = jnp.zeros_like(acc2_ref)
        accp_ref[...] = jnp.zeros_like(accp_ref)
        vec_ref[...] = jnp.zeros_like(vec_ref)
        weights("wait")
        for r in range(4):
            wp_ref[:, r * pq : (r + 1) * pq] = all_ref[:, r * quarter : r * quarter + pq]
        at = pq + hidden // 4
        for shard in range(width // rps):
            for b in range(per):
                to = (shard * per + b) * rps
                w2_ref[to : to + rps, :] = all_ref[
                    shard * rps : (shard + 1) * rps, b * quarter + at : b * quarter + at + width
                ]

    o, y = o_ref[...], y_ref[...]
    r1 = x_ref[...].astype(F32) + dot(o, wp_ref[...])
    n, rstd = normed(r1)
    gain = vector(slots_ref, 3, nslot)
    h = (n * gain + vector(slots_ref, 4, nslot)).astype(BF)
    ht = h.T
    out = r1 + vector(slots_ref, 0, nslot)
    dh = jnp.zeros_like(r1)
    for j in range(per):
        at = slice(j * width, (j + 1) * width)
        w1 = all_ref[:, j * quarter + pq : j * quarter + pq + width]
        u = dot(h, w1) + vector(slots_ref, 5 + j, nslot)
        da = dot_nt(y, w2_ref[at, :])
        cdf = 0.5 + 0.5 * lax.erf(u * 0.7071067811865476)
        pdf = jnp.exp(u * u * -0.5) * 0.3989422804014327
        a = (u * cdf).astype(BF)
        du = (da * (cdf + u * pdf)).astype(BF)
        out += dot(a, w2_ref[at, :])
        dh += dot_nt(du, w1)
        acc1_ref[:, at] += dot(ht, du)
        acc2_ref[at, :] += dot_tn(a, y)
        vec_ref[0:1, at] += jnp.sum(du.astype(F32), axis=0, keepdims=True)
    out_ref[...] = out
    yf = y.astype(F32)
    dr = yf + norm_back(dh * gain, n, rstd)
    dr_ref[...] = dr
    accp_ref[...] += dot_tn(o, dr.astype(BF))
    vec_ref[1:2, :width] += jnp.sum(yf, axis=0, keepdims=True)
    vec_ref[2:3, :width] += jnp.sum(dh * n, axis=0, keepdims=True)
    vec_ref[3:4, :width] += jnp.sum(dh, axis=0, keepdims=True)

    @pl.when(step == pl.num_programs(0) - 1)
    def _():
        for which, ref in ((0, keep_ref), (1, send_ref)):
            half = meta[2] if which == 0 else 1 - meta[2]
            pcol = pl.ds(pl.multiple_of(half * ph, 128), ph)
            ref[:, :ph] = accp_ref[:, pcol].astype(BF)
            ref[:, ph : ph + wh] = acc1_ref[:, pl.ds(pl.multiple_of(half * wh, 128), wh)].astype(BF)
            for shard in range(width // rps):
                for j in range(per):
                    at = (shard * per + j) * rps
                    ref[shard * rps : (shard + 1) * rps, ph + wh + j * ph : ph + wh + (j + 1) * ph] = (
                        acc2_ref[at : at + rps, pcol].astype(BF)
                    )


def back_kernel(meta, *refs, sizes, seqs, span, start, begin, end):
    (
        dr_ref,
        x_ref,
        qkv_ref,
        lse_ref,
        w_ref,
        wp_ref,
        slots_ref,
        from_ref,
        pbias_ref,
    ) = refs[:9]
    rest = refs[9:]
    if not begin:
        sum_ref, rest = rest[0], rest[3:]
    if end:
        dqkv_ref, dpool_ref, keep_ref, send_ref, vec_ref, acc_ref, dkvb_ref = rest
    else:
        dqkv_ref, dpool_ref, acc_ref, dkvb_ref = rest
    width = x_ref.shape[1]
    scale = (width // HEADS) ** -0.5
    step = pl.program_id(0)

    @pl.when(step == 0)
    def _():
        acc_ref[...] = jnp.zeros_like(acc_ref) if begin else sum_ref[...]

    nslot = pbias_ref.shape[1]
    cp = -(-nslot // 16) * 16
    gain, shift = vector(slots_ref, 1, nslot), vector(slots_ref, 2, nslot)
    seq0 = step * seqs + start
    pool = jnp.concatenate(
        [pooled_tokens(meta, slots_ref, seq0 + i, sizes, cp) for i in range(seqs)], axis=0
    )
    pooled_h = (pool * gain + shift).astype(BF)
    kvb = dot(pooled_h, w_ref[:, width:]).astype(BF)
    dr = dr_ref[...]
    do = dot_nt(dr.astype(BF), wp_ref[...]).astype(BF)
    pairs = range(HEADS // 2)
    col = lambda part, p: slice(part * width + p * 128, part * width + (p + 1) * 128)
    for s in range(seqs):
        rows = slice(s * span, (s + 1) * span)
        prow = slice(s * cp, (s + 1) * cp)
        bias = span_bias(from_ref[s], padded(pbias_ref[s], cp, masked))
        both = lambda part, p: jnp.concatenate(
            [qkv_ref[rows, col(part, p)], kvb[prow, col(part - 1, p)]], axis=0
        )
        q = [qkv_ref[rows, col(0, p)] for p in pairs]
        g = [do[rows, col(0, p)] for p in pairs]
        keys = [both(1, p) for p in pairs]
        scores = [dot(keys[p], two_heads_lanes(q[p].T)) + bias for p in pairs]
        dprob = [dot(both(2, p), two_heads_lanes(g[p].T)) for p in pairs]
        prob = [jnp.exp(scores[p] - lse_ref[s, p : p + 1, :]) for p in pairs]
        weighted = [prob[p] * dprob[p] for p in pairs]
        ds = [
            (weighted[p] - prob[p] * jnp.sum(weighted[p], axis=0, keepdims=True)).astype(BF)
            for p in pairs
        ]
        dv = [dot(prob[p].astype(BF), two_heads_rows(g[p])).astype(BF) for p in pairs]
        dq = [(diagonal(dot_tn(keys[p], ds[p])) * scale).astype(BF) for p in pairs]
        dk = [dot(ds[p], two_heads_rows(q[p])).astype(BF) for p in pairs]
        for p in pairs:
            dqkv_ref[rows, col(0, p)] = dq[p].T
            dqkv_ref[rows, col(1, p)] = dk[p][:span]
            dqkv_ref[rows, col(2, p)] = dv[p][:span]
            dkvb_ref[prow, col(0, p)] = dk[p][span:]
            dkvb_ref[prow, col(1, p)] = dv[p][span:]
    n, _ = normed(x_ref[...].astype(F32))
    h = (n * gain + shift).astype(BF)
    dqkv, dkvb = dqkv_ref[...], dkvb_ref[...]
    acc_ref[:width] += dot_tn(h, dqkv)
    acc_ref[:width, width:] += dot_tn(pooled_h, dkvb)
    acc_ref[width : width + 1] += jnp.sum(dqkv.astype(F32), axis=0, keepdims=True)
    acc_ref[width : width + 1, width:] += jnp.sum(dkvb.astype(F32), axis=0, keepdims=True)
    dpool_ref[...] = dot_nt(dkvb, w_ref[:, width:]).astype(BF).reshape(seqs, cp, width)
    if not end:
        return

    @pl.when(step == pl.num_programs(0) - 1)
    def _():
        nh = acc_ref.shape[1] // 2
        for which, ref in ((0, keep_ref), (1, send_ref)):
            half = meta[2] if which == 0 else 1 - meta[2]
            ref[...] = acc_ref[:width, pl.ds(pl.multiple_of(half * nh, 128), nh)].astype(BF)
        w = w_ref[...].astype(F32)

        def row(m):
            total = jnp.sum(m, axis=1, keepdims=True)
            return jnp.broadcast_to(total, (width, 128)).T[:1]

        dshift = row(w * acc_ref[width : width + 1])
        dgain = (row(w * acc_ref[:width]) - shift * dshift) / gain
        vec_ref[0:1] = dgain
        vec_ref[1:2] = dshift


def last_kernel(meta, len_ref, dr_ref, x_ref, dqkv_ref, w_ref, dpool_ref, slots_ref, out_ref, *, seqs, span, nslot):
    n, rstd = normed(x_ref[...].astype(F32))
    dh = dot_nt(dqkv_ref[...], w_ref[...])
    for i in range(seqs):
        starts = doc_starts(len_ref, pl.program_id(0) * seqs + i)
        first = first_member(starts, (meta[0] * meta[4] + meta[1]) * span, span)
        rows = slice(i * span, (i + 1) * span)
        count = jnp.full((1, 1), span - first, jnp.int32).astype(F32)
        share = dpool_ref[i] / count
        row = lax.broadcasted_iota(jnp.int32, (span, n.shape[1]), 0)
        e = (dh[rows] + jnp.where(row >= first, share, 0.0)) * vector(slots_ref, 1, nslot)
        out_ref[rows, :] = dr_ref[rows, :] + norm_back(e, n[rows], rstd[rows])


def after(a, *first):
    return lax.optimization_barrier((a, *first))[0]


def params(mib):
    return pltpu.CompilerParams(dimension_semantics=("arbitrary",), vmem_limit_bytes=mib * MIB)


LITTLE = pl.CostEstimate(flops=1, bytes_accessed=1, transcendentals=0)


def local(
    tokens,
    cotangent,
    doc_lengths,
    attend,
    project,
    widen,
    narrow,
    hidden_bias,
    final_bias,
    gain_first,
    shift_first,
    gain_second,
    shift_second,
    *,
    sizes,
):
    zs, xs, ys, cs = sizes
    nshard = zs * xs
    seq_count, span, width = tokens.shape
    rows = seq_count * span
    hidden = widen.shape[1]
    rps = attend.shape[0]
    rep, shard = lax.axis_index("rep"), lax.axis_index("shard")
    z, x, y, core = shard // xs, shard % xs, rep // cs, rep % cs
    meta = jnp.stack([z, x, core, y % 2, jnp.int32(xs)]).astype(jnp.int32)

    def swap(a, z=0, x=0, y=0, c=0):
        perm = []
        for r in range(ys * cs):
            for s in range(nshard):
                r2 = (r // cs ^ y) * cs + (r % cs ^ c)
                s2 = (s // xs ^ z) * xs + (s % xs ^ x)
                perm.append((r * nshard + s, r2 * nshard + s2))
        return lax.ppermute(a, ("rep", "shard"), perm)

    bits = lambda n: [1 << i for i in range(n.bit_length() - 1)]

    def send(a, dz=0, dx=0, dy=0, dc=0):
        perm = []
        for r in range(ys * cs):
            for s in range(nshard):
                r2 = (r // cs + dy) % ys * cs + (r % cs + dc) % cs
                s2 = (s // xs + dz) % zs * xs + (s % xs + dx) % xs
                perm.append((r * nshard + s, r2 * nshard + s2))
        return lax.ppermute(a, ("rep", "shard"), perm)

    def levels(a):
        return jnp.concatenate([a] + [swap(a, z=k) for k in range(1, zs)], axis=0)

    def sides(a):
        return [a] + [swap(a, x=k) for k in range(1, xs)]

    x2 = tokens.reshape(rows, width)
    y2 = cotangent.reshape(rows, width)
    smem = pl.BlockSpec(memory_space=pltpu.SMEM)
    hbm = pl.BlockSpec(memory_space=pl.ANY)
    nh = attend.shape[1] // 2
    per = hidden // width
    hs = hidden_bias.shape[0]
    attend_col = levels(lax.dynamic_slice_in_dim(attend, core * nh, nh, 1))

    small = jnp.stack([final_bias, gain_first, shift_first, gain_second, shift_second])
    total = seq_count + 5 + 4
    pool_seqs = 8
    packed, doc_from, pbias = pl.pallas_call(
        functools.partial(prep_kernel, sizes=(zs, xs), seqs=pool_seqs),
        grid=(seq_count // pool_seqs,),
        in_specs=[
            smem,
            smem,
            pl.BlockSpec((pool_seqs * span, width), lambda i: (i, 0)),
            pl.BlockSpec((5, rps), lambda i: (0, 0)),
            pl.BlockSpec((1, hs), lambda i: (0, 0)),
        ],
        out_specs=[
            pl.BlockSpec((total, width), lambda i: (0, 0)),
            pl.BlockSpec((pool_seqs, 1, span), lambda i: (i, 0, 0)),
            pl.BlockSpec((pool_seqs, nshard, span), lambda i: (i, 0, 0)),
        ],
        out_shape=[
            jax.ShapeDtypeStruct((total, width), F32),
            jax.ShapeDtypeStruct((seq_count, 1, span), jnp.int32),
            jax.ShapeDtypeStruct((seq_count, nshard, span), F32),
        ],
        compiler_params=params(58),
        cost_estimate=LITTLE,
        name="prep",
    )(meta, doc_lengths, x2, small, hidden_bias[None])
    slots = packed
    for b in bits(zs):
        slots = jnp.concatenate([slots, swap(slots, z=b)], axis=0)
    for b in bits(xs):
        slots = jnp.concatenate([slots, swap(slots, x=b)], axis=0)

    ph, wh = width // 2, hidden // 2
    pair = y % 2
    mine = pair * 2 + core
    cut = lambda a, axis: lax.dynamic_slice_in_dim(
        a, mine * (a.shape[axis] // 4), a.shape[axis] // 4, axis
    )
    ffn_own = jnp.concatenate([cut(project, 1), cut(widen, 1), cut(narrow, 0)], axis=1)
    attend_cols = sides(attend_col)
    attend_parts = attend_cols + [swap(m, c=1) for m in attend_cols]
    ffn_col = levels(after(ffn_own, attend_col)).reshape(zs, rps, -1)
    kr = rps // 2
    over_xs = [ffn_col[:, :kr].reshape(zs * kr, -1)]
    for b in bits(xs):
        over_xs.append(swap(jnp.concatenate(over_xs, axis=0), x=b))
    over_ys = [ffn_col[:, kr:].reshape(zs * kr, -1)]
    over_ys.append(swap(over_ys[0], y=1))

    seqs = 4
    calls = 2
    steps = seq_count // seqs // calls
    all_spec = lambda a, b: pl.BlockSpec((a, b), lambda i, m: (0, 0))
    row_spec = lambda n, w, c=0: pl.BlockSpec((n, w), lambda i, m: (i + c * steps, 0))
    seq_spec = lambda n, a, b, c=0: pl.BlockSpec((n, a, b), lambda i, m: (i + c * steps, 0, 0))
    act_specs = lambda c: [
        row_spec(seqs * span, 3 * width, c),
        row_spec(seqs * span, width, c),
        seq_spec(seqs, HEADS // 2, 2 * span, c),
    ]
    act_shapes = [
        jax.ShapeDtypeStruct((rows, 3 * width), BF),
        jax.ShapeDtypeStruct((rows, width), BF),
        jax.ShapeDtypeStruct((seq_count, HEADS // 2, 2 * span), F32),
    ]

    def attention(c, x2, weights, before):
        return pl.pallas_call(
            functools.partial(
                attend_kernel,
                sizes=(zs, xs),
                seqs=seqs,
                span=span,
                rps=rps,
                start=c * steps * seqs,
            ),
            grid_spec=pltpu.PrefetchScalarGridSpec(
                num_scalar_prefetch=1,
                grid=(steps,),
                in_specs=[
                    row_spec(seqs * span, width, c),
                    all_spec(nshard * total, width),
                    seq_spec(seqs, 1, span, c),
                    seq_spec(seqs, nshard, span, c),
                ]
                + ([all_spec(width, 3 * width)] if c else [hbm] * len(weights))
                + [hbm] * len(before),
                out_specs=([] if c else [all_spec(width, 3 * width)]) + act_specs(c),
                scratch_shapes=[] if c else [pltpu.SemaphoreType.DMA((1, 2 * nshard))],
            ),
            out_shape=([] if c else [jax.ShapeDtypeStruct((width, 3 * width), BF)]) + act_shapes,
            input_output_aliases={6 + i: i for i in range(len(before))},
            compiler_params=params(58),
            cost_estimate=LITTLE,
            name="attention",
        )(meta, x2, slots, doc_from, pbias, *weights, *before)

    w_all, qkv, o, lse = attention(0, after(x2, ffn_col), attend_parts, [])
    over_xs, over_ys = after(over_xs, lse), after(over_ys, lse)
    if len(over_xs) > 1:
        over_xs = [jnp.concatenate(over_xs, axis=0)]
    over_ys = [jnp.concatenate(over_ys, axis=0)]
    both = [over_xs[0], over_ys[0]]
    both_other = [swap(a, c=1) for a in both]
    ends = [swap(over_xs[0], y=1)]
    so_far = over_ys
    for b in bits(xs):
        so_far.append(swap(jnp.concatenate(so_far, axis=0), x=b))
    ends += so_far[1:]
    qkv, o, lse = attention(1, after(x2, *both), [w_all], [qkv, o, lse])
    ends = after(ends, lse)
    ffn_parts = both + both_other + ends + [swap(a, c=1) for a in ends]
    two = [[(kx, 0, 0) for kx in range(xs)], [(0, ky, kr) for ky in range(2)]]
    rest = [[(kx, 1, 0) for kx in range(xs)]]
    rest += [[(kx, ky, kr) for kx in range(b, 2 * b) for ky in range(2)] for b in bits(xs)]
    places = [
        [
            ((i * zs + kz) * kr, kr, kz, kx, ky, kc, part)
            for i, (kx, ky, part) in enumerate(units)
            for kz in range(zs)
        ]
        for group in (two, rest)
        for kc in range(2)
        for units in group
    ]

    tile = 512
    packet = ph + wh + per * ph
    steps, cp = 0, -(-nshard // 16) * 16
    block_out, dr, keep_f, send_f, wp_all, vec_f = pl.pallas_call(
        functools.partial(ffn_kernel, rps=rps, places=places, nslot=nshard),
        grid_spec=pltpu.PrefetchScalarGridSpec(
            num_scalar_prefetch=1,
            grid=(rows // tile,),
            in_specs=[
                row_spec(tile, width),
                row_spec(tile, width),
                row_spec(tile, width),
                all_spec(nshard * total, width),
            ]
            + [hbm] * len(ffn_parts),
            out_specs=[
                row_spec(tile, width),
                row_spec(tile, width),
                all_spec(width, packet),
                all_spec(width, packet),
                all_spec(width, width),
                all_spec(8, hidden),
            ],
            scratch_shapes=[
                pltpu.VMEM((width, width + 2 * hidden), BF),
                pltpu.VMEM((hidden, width), BF),
                pltpu.VMEM((width, hidden), F32),
                pltpu.VMEM((hidden, width), F32),
                pltpu.VMEM((width, width), F32),
                pltpu.SemaphoreType.DMA((sum(len(p) for p in places),)),
            ],
        ),
        out_shape=[
            jax.ShapeDtypeStruct((rows, width), F32),
            jax.ShapeDtypeStruct((rows, width), F32),
            jax.ShapeDtypeStruct((width, packet), BF),
            jax.ShapeDtypeStruct((width, packet), BF),
            jax.ShapeDtypeStruct((width, width), BF),
            jax.ShapeDtypeStruct((8, hidden), F32),
        ],
        compiler_params=params(58),
        cost_estimate=LITTLE,
        name="ffn",
    )(meta, o, x2, y2, slots, *ffn_parts)

    def add(parts, kind):
        total = parts[0].astype(F32)
        for p in parts[1:]:
            total = total + p.astype(F32)
        return total.astype(kind)

    def over_x(a, cover):
        piece = lambda dx: lax.dynamic_slice_in_dim(a, (x + dx) % xs, 1, 1)
        parts = [send(piece(dx), dx=dx) if dx else piece(0) for dx in range(xs)]
        return add(after(parts, cover), BF)

    def over_y(a, cover):
        n = a.shape[-1] // ys
        piece = lambda dy: lax.dynamic_slice_in_dim(a, (y + dy) % ys * n, n, a.ndim - 1)
        parts = [send(piece(dy), dy=dy) if dy else piece(0) for dy in range(ys)]
        return add(after(parts, cover), BF)

    def over_z(a, cover):
        k = a.shape[0] // zs
        piece = lambda dz: lax.dynamic_slice_in_dim(a, (z + dz) % zs * k, k, 0)
        parts = [send(piece(dz), dz=dz) if dz else piece(0) for dz in range(zs)]
        return add(after(parts, cover), BF)

    def over_xy(part):
        n = part.shape[1] // ys
        k = part.shape[0] // nshard
        view = part.reshape(zs, xs, k, ys * n)

        def corner(dx, dy):
            at = (0, (x + dx) % xs, 0, (y + dy) % ys * n)
            return lax.dynamic_slice(view, at, (zs, 1, k, n)).reshape(zs * k, n)

        parts = [
            send(corner(dx, dy), dx=dx, dy=dy) if dx or dy else corner(0, 0)
            for dx in range(xs)
            for dy in range(ys)
        ]
        return add(parts, BF)

    def replicas(part):
        found = {
            (dy, dc): send(part, dy=dy, dc=dc) if dy or dc else part
            for dy in range(ys)
            for dc in range(cs)
        }
        total = []
        for at in range(ys * cs):
            picked = jnp.zeros(part.shape, F32)
            for (dy, dc), piece in found.items():
                mine = ((y - dy + ys) % ys == at % ys) & ((core - dc + cs) % cs == at // ys)
                picked = jnp.where(mine, piece.astype(F32), picked)
            total.append(picked)
        return total

    total_steps = seq_count // seqs
    cuts = [0, total_steps // 4, total_steps * 3 // 4, total_steps]

    def back(c, dr, before):
        first_step = cuts[c]
        end = c == 2
        row_spec = lambda n, w: pl.BlockSpec((n, w), lambda i, m: (i + first_step, 0))
        seq_spec = lambda n, a, b: pl.BlockSpec((n, a, b), lambda i, m: (i + first_step, 0, 0))
        nacc = width + 8
        sums = [all_spec(nacc, 3 * width)]
        halves = [all_spec(width, 3 * width // 2)] * 2 + [all_spec(8, width)]
        half_shapes = [
            jax.ShapeDtypeStruct((width, 3 * width // 2), BF),
            jax.ShapeDtypeStruct((width, 3 * width // 2), BF),
            jax.ShapeDtypeStruct((8, width), F32),
        ]
        return pl.pallas_call(
            functools.partial(
                back_kernel,
                sizes=(zs, xs),
                seqs=seqs,
                span=span,
                start=first_step * seqs,
                begin=c == 0,
                end=end,
            ),
            grid_spec=pltpu.PrefetchScalarGridSpec(
                num_scalar_prefetch=1,
                grid=(cuts[c + 1] - first_step,),
                in_specs=[
                    row_spec(seqs * span, width),
                    row_spec(seqs * span, width),
                    row_spec(seqs * span, 3 * width),
                    seq_spec(seqs, HEADS // 2, 2 * span),
                    all_spec(width, 3 * width),
                    all_spec(width, width),
                    all_spec(nshard * total, width),
                    seq_spec(seqs, 1, span),
                    seq_spec(seqs, nshard, span),
                ]
                + ((sums + [hbm, hbm]) if c else []),
                out_specs=[row_spec(seqs * span, 3 * width), seq_spec(seqs, cp, width)]
                + (halves if end else sums),
                scratch_shapes=([pltpu.VMEM((nacc, 3 * width), F32)] if end else [])
                + [pltpu.VMEM((seqs * cp, 2 * width), BF)],
            ),
            out_shape=[
                jax.ShapeDtypeStruct((rows, 3 * width), BF),
                jax.ShapeDtypeStruct((seq_count, cp, width), BF),
            ]
            + (half_shapes if end else [jax.ShapeDtypeStruct((nacc, 3 * width), F32)]),
            input_output_aliases={11: 0, 12: 1} if c else {},
            compiler_params=params(58),
            cost_estimate=LITTLE,
            name="back",
        )(meta, dr, x2, qkv, lse, w_all, wp_all, slots, doc_from, pbias, *before)

    dqkv, dpool, sums = back(0, dr, [])
    part_f = add([keep_f, after(send(send_f, dc=1), sums)], BF)
    dqkv, dpool, sums = back(1, after(dr, part_f), [sums, dqkv, dpool])
    kf = part_f.shape[0] // nshard
    view = part_f.reshape(zs, xs, kf, packet)
    first_f = over_x(view[:, :, : kf // 2], sums)
    second_f = over_y(view[:, :, kf // 2 :], sums)
    dqkv, dpool, keep_a, send_a, vec_a = back(
        2, after(dr, first_f, second_f), [sums, dqkv, dpool]
    )
    part_a = add([keep_a, send(send_a, dc=1)], BF)
    part_f = jnp.concatenate([over_y(first_f, vec_a), over_x(second_f, vec_a)], axis=2)
    part_f = part_f.reshape(zs * kf, packet // ys)
    share_a = over_xy(part_a)
    zbits = list(reversed(bits(zs)))
    share_f = part_f
    last_parts = None
    for b in zbits:
        n = share_f.shape[0] // 2
        upper = (z // b) % 2
        kept = lax.dynamic_slice_in_dim(share_f, upper * n, n, 0)
        other = swap(lax.dynamic_slice_in_dim(share_f, (1 - upper) * n, n, 0), z=b)
        if b == 1:
            last_parts = [kept, other]
        else:
            share_f = add([kept, after(other, share_a)], BF)

    vec = jnp.concatenate(
        [vec_f[0].reshape(per, width), vec_f[1:2, :width], vec_a[:2], vec_f[2:4, :width]], axis=0
    ).astype(BF)
    nvec = vec.shape[0]
    dp = jnp.transpose(after(dpool, part_a, part_f)[:, :nshard], (1, 0, 2))
    dp = jnp.concatenate([dp, jnp.broadcast_to(vec, (nshard, nvec, width))], axis=1)
    dp = lax.all_to_all(dp, "shard", 0, 0, tiled=True)
    own = jnp.sum(dp.astype(F32), axis=0)
    own_vec = jnp.concatenate(
        [lax.dynamic_slice(own[seq_count:].reshape(nvec * width), (shard * hs,), (hs,))]
        + [
            lax.dynamic_slice(own[seq_count + per + i], (shard * rps,), (rps,))
            for i in range(5)
        ]
    ).astype(BF)
    tokens_grad = pl.pallas_call(
        functools.partial(last_kernel, seqs=seqs, span=span, nslot=nshard),
        grid=(seq_count // seqs,),
        in_specs=[
            smem,
            smem,
            pl.BlockSpec((seqs * span, width), lambda i: (i, 0)),
            pl.BlockSpec((seqs * span, width), lambda i: (i, 0)),
            pl.BlockSpec((seqs * span, 3 * width), lambda i: (i, 0)),
            pl.BlockSpec((width, 3 * width), lambda i: (0, 0)),
            pl.BlockSpec((seqs, 1, width), lambda i: (i, 0, 0)),
            pl.BlockSpec((nshard * total, width), lambda i: (0, 0)),
        ],
        out_specs=pl.BlockSpec((seqs * span, width), lambda i: (i, 0)),
        out_shape=jax.ShapeDtypeStruct((rows, width), F32),
        compiler_params=params(58),
        cost_estimate=LITTLE,
        name="last",
    )(
        meta,
        doc_lengths,
        after(dr, share_a, share_f),
        x2,
        dqkv,
        w_all,
        own[:seq_count].reshape(seq_count, 1, width),
        slots,
    )

    share_a = over_z(share_a, tokens_grad)
    share_f = add(after(last_parts, tokens_grad), BF)
    na, nf = share_a.shape[1], share_f.shape[1]
    vrows = -(-own_vec.shape[0] // (na + nf))
    own_vec = jnp.pad(own_vec, (0, vrows * (na + nf) - own_vec.shape[0]))
    found = replicas(
        jnp.concatenate(
            [
                jnp.concatenate([share_a, share_f], axis=1),
                own_vec.reshape(vrows, na + nf),
            ],
            axis=0,
        )
    )
    grad_attend = jnp.concatenate([f[:rps, :na] for f in found], axis=1)
    grad_f = jnp.concatenate([f[:rps, na:] for f in found], axis=1)
    halves = [grad_f[:, i * packet : (i + 1) * packet] for i in range(2)]
    grad_project = jnp.concatenate([h[:, :ph] for h in halves], axis=1)
    grad_widen = jnp.concatenate([h[:, ph : ph + wh] for h in halves], axis=1)
    grad_narrow = jnp.concatenate(
        [
            jnp.concatenate(
                [h[:, ph + wh + j * ph : ph + wh + (j + 1) * ph] for h in halves], axis=1
            )
            for j in range(per)
        ],
        axis=0,
    )
    vec = sum(f[rps:] for f in found).reshape(vrows * (na + nf))
    vecs = [vec[:hs]] + [vec[hs + i * rps : hs + (i + 1) * rps] for i in range(5)]
    return (
        block_out.reshape(tokens.shape),
        tokens_grad.reshape(tokens.shape),
        grad_attend,
        grad_project,
        grad_widen,
        grad_narrow,
        *vecs,
    )


def solution(mesh):
    first = mesh.devices[0]
    xs = len({d.coords[0] for d in first})
    cs = len({d.core_on_chip for d in mesh.devices[:, 0]})
    sizes = (mesh.shape["shard"] // xs, xs, mesh.shape["rep"] // cs, cs)
    row = P("shard", None)
    vec = P("shard")
    act = P("rep", "shard", None)
    return jax.shard_map(
        functools.partial(local, sizes=sizes),
        mesh=mesh,
        in_specs=(act, act, P("rep", None), row, row, row, row) + (vec,) * 6,
        out_specs=(act, act, row, row, row, row) + (vec,) * 6,
        check_vma=False,
    )
```

```python
import functools

import jax
import jax.numpy as jnp
from jax import lax
from jax.experimental import pallas as pl
from jax.experimental.pallas import tpu as pltpu
from jax.sharding import PartitionSpec as P

HEADS = 8
epsilon = 1e-05
masked = -1e30
F32 = jnp.float32
BF = jnp.bfloat16
MIB = 1 << 20


def dot(a, b):
    return jnp.dot(a, b, preferred_element_type=F32)


def dot_nt(a, b):
    return lax.dot_general(a, b, (((1,), (1,)), ((), ())), preferred_element_type=F32)


def dot_tn(a, b):
    return lax.dot_general(a, b, (((0,), (0,)), ((), ())), preferred_element_type=F32)


def normed(v):
    center = v - jnp.mean(v, axis=-1, keepdims=True)
    rstd = lax.rsqrt(jnp.mean(center * center, axis=-1, keepdims=True) + epsilon)
    return center * rstd, rstd


def norm_back(e, n, rstd):
    return rstd * (
        e - jnp.mean(e, axis=-1, keepdims=True) - n * jnp.mean(e * n, axis=-1, keepdims=True)
    )


def two_heads_lanes(t):
    half = t.shape[0] // 2
    zero = jnp.zeros((half, t.shape[1]), t.dtype)
    left = jnp.concatenate([t[:half], zero], axis=0)
    right = jnp.concatenate([zero, t[half:]], axis=0)
    return jnp.concatenate([left, right], axis=1)


def two_heads_rows(a):
    first = lax.broadcasted_iota(jnp.int32, a.shape, 1) < a.shape[1] // 2
    zero = jnp.zeros_like(a)
    return jnp.concatenate([jnp.where(first, a, zero), jnp.where(first, zero, a)], axis=0)


def diagonal(t):
    rows, cols = t.shape[0] // 2, t.shape[1] // 2
    return jnp.concatenate([t[:rows, :cols], t[rows:, cols:]], axis=0)


def span_bias(doc_from, pooled):
    span = doc_from.shape[1]
    key = lax.broadcasted_iota(jnp.int32, (span, span), 0)
    query = lax.broadcasted_iota(jnp.int32, (span, span), 1)
    direct = jnp.where((key >= doc_from) & (key <= query), 0.0, masked).astype(F32)
    both = jnp.concatenate([direct, pooled], axis=0)
    return jnp.concatenate([both, both], axis=1)


def arriving(meta, sizes, pieces, places, sems, act, kind):
    zs, xs = sizes
    z, x, core = meta[0], meta[1], meta[2]
    at = 0
    for which in range(2):
        half = core if which == 0 else 1 - core
        for kx in range(xs):
            for kz in range(zs):
                shard = (z ^ kz) * xs + (x ^ kx)
                for src, dst in places[kind](pieces, which, kx, kz, shard, half):
                    copy = pltpu.make_async_copy(src, dst, sems.at[kind, at])
                    copy.start() if act == "start" else copy.wait()
                    at += 1


def doc_starts(len_ref, seq):
    starts = [jnp.int32(0)]
    for j in range(len_ref.shape[1] - 1):
        starts.append(starts[-1] + len_ref[seq, j])
    return starts


def start_at(starts, position):
    found = jnp.zeros_like(position)
    for start in starts:
        found = jnp.where(position >= start, start, found)
    return found


def first_member(starts, base, span):
    return jnp.maximum(start_at(starts, base + span - 1) - base, 0)


def prep_kernel(meta, len_ref, x_ref, small_ref, hidden_ref, out_ref, from_ref, pbias_ref, *, sizes, seqs):
    zs, xs = sizes
    z, x = meta[0], meta[1]
    shard = z * xs + x
    nshard, span = pbias_ref.shape[1:]
    width = x_ref.shape[1]
    total = out_ref.shape[0] - small_ref.shape[0] - 4
    step = pl.program_id(0)
    base = shard * span

    @pl.when(step == 0)
    def _():
        def place(v, at):
            row = lax.broadcasted_iota(jnp.int32, (v.shape[1], width), 0)
            lane = lax.broadcasted_iota(jnp.int32, (v.shape[1], width), 1)
            return dot(v, (lane == row + at).astype(F32).astype(BF))

        nsmall, n = small_ref.shape
        rows = [place(small_ref[...], shard * n)]
        for r in range(4):
            rows.append(place(hidden_ref[...], shard * hidden_ref.shape[1] - r * width))
        out_ref[total:, :] = jnp.concatenate(rows, axis=0)

    n, _ = normed(x_ref[...].astype(F32))
    row = lax.broadcasted_iota(jnp.int32, (span, width), 0)
    slot = lax.broadcasted_iota(jnp.int32, (nshard, span), 0)
    slot_span = (z ^ (slot & (zs - 1))) * xs + (x ^ (slot // zs))
    slot_last = slot_span * span + span - 1
    position = base + lax.broadcasted_iota(jnp.int32, (1, span), 1)
    pooled = []
    for i in range(seqs):
        starts = doc_starts(len_ref, step * seqs + i)
        first = first_member(starts, base, span)
        part = jnp.where(row >= first, n[i * span : (i + 1) * span], 0.0)
        count = jnp.full((1, 1), span - first, jnp.int32).astype(F32)
        pooled.append(jnp.sum(part, axis=0, keepdims=True) / count)
        here = start_at(starts, position)
        from_ref[i] = here - base
        last = start_at(starts, slot_last)
        counts = jnp.minimum(span, slot_last + 1 - last).astype(F32)
        seen = (slot_span < shard) & (last == here)
        pbias_ref[i] = jnp.where(seen, jnp.log(counts), masked)
    at = pl.multiple_of(step * seqs, seqs)
    out_ref[pl.ds(at, seqs), :] = jnp.concatenate(pooled, axis=0)


def padded(a, rows, value):
    shape = a.shape[:-2] + (rows - a.shape[-2], a.shape[-1])
    return jnp.concatenate([a, jnp.full(shape, value, a.dtype)], axis=-2) if shape[-2] else a


def vector(slots_ref, i, nslot):
    total = slots_ref.shape[0] // nslot
    at = [k * total + total - 9 + i for k in range(nslot)]
    return sum(slots_ref[k : k + 1, :] for k in at)


def pooled_tokens(slots_ref, seq, nslot, cp):
    total = slots_ref.shape[0] // nslot
    rows = [slots_ref[pl.ds(k * total + seq, 1), :] for k in range(nslot)]
    return padded(jnp.concatenate(rows, axis=0), cp, 0.0)


def attend_kernel(meta, *refs, sizes, seqs, span, rps, start):
    x_ref, slots_ref, from_ref, pbias_ref = refs[:4]
    width = x_ref.shape[1]
    nslot = pbias_ref.shape[1]
    cp = -(-nslot // 16) * 16
    gain, shift = vector(slots_ref, 1, nslot), vector(slots_ref, 2, nslot)
    seq0 = pl.program_id(0) * seqs + start
    if start:
        w_ref, _, _, _, qkv_ref, o_ref, lse_ref = refs[4:]
    else:
        xs = sizes[1]
        pieces = refs[4 : 4 + 2 * xs]
        w_ref, qkv_ref, o_ref, lse_ref, sems = refs[4 + 2 * xs :]
        nh = w_ref.shape[1] // 2

        def place(pieces, which, kx, kz, shard, half):
            yield (
                pieces[which * xs + kx].at[pl.ds(kz * rps, rps), :],
                w_ref.at[
                    pl.ds(pl.multiple_of(shard * rps, rps), rps),
                    pl.ds(pl.multiple_of(half * nh, 128), nh),
                ],
            )

        @pl.when(pl.program_id(0) == 0)
        def _():
            arriving(meta, sizes, pieces, [place], sems, "start", 0)

    n, _ = normed(x_ref[...].astype(F32))
    h = (n * gain + shift).astype(BF)
    pooled_h = jnp.concatenate(
        [pooled_tokens(slots_ref, seq0 + i, nslot, cp) for i in range(seqs)], axis=0
    )
    pooled_h = pooled_h * gain + shift
    if not start:

        @pl.when(pl.program_id(0) == 0)
        def _():
            arriving(meta, sizes, pieces, [place], sems, "wait", 0)

    qkv = dot(h, w_ref[...]).astype(BF)
    q = qkv[:, :width] * jnp.asarray((width // HEADS) ** -0.5, BF)
    qkv_ref[:, :width] = q
    qkv_ref[:, width:] = qkv[:, width:]
    kvb = dot(pooled_h.astype(BF), w_ref[:, width:]).astype(BF)
    pairs = range(HEADS // 2)
    col = lambda part, p: slice(part * width + p * 128, part * width + (p + 1) * 128)
    for s in range(seqs):
        rows = slice(s * span, (s + 1) * span)
        prow = slice(s * cp, (s + 1) * cp)
        bias = span_bias(from_ref[s], padded(pbias_ref[s], cp, masked))
        both = lambda part, p: jnp.concatenate(
            [qkv[rows, col(part, p)], kvb[prow, col(part - 1, p)]], axis=0
        )
        query = [two_heads_lanes(q[rows, col(0, p)].T) for p in pairs]
        scores = [dot(both(1, p), query[p]) + bias for p in pairs]
        top = [jnp.max(scores[p], axis=0, keepdims=True) for p in pairs]
        e = [jnp.exp(scores[p] - top[p]) for p in pairs]
        total = [jnp.sum(e[p], axis=0, keepdims=True) for p in pairs]
        prob = [(e[p] * (1.0 / total[p])).astype(BF) for p in pairs]
        out = [diagonal(dot_tn(both(2, p), prob[p])).astype(BF) for p in pairs]
        for p in pairs:
            lse_ref[s, p : p + 1, :] = top[p] + jnp.log(total[p])
            o_ref[rows, col(0, p)] = out[p].T


def ffn_kernel(meta, *refs, rps, places, nslot):
    o_ref, x_ref, y_ref, slots_ref = refs[:4]
    pieces = refs[4 : 4 + len(places)]
    (
        out_ref,
        dr_ref,
        keep_ref,
        send_ref,
        wp_ref,
        vec_ref,
        all_ref,
        w2_ref,
        acc1_ref,
        acc2_ref,
        accp_ref,
        sems,
    ) = refs[4 + len(places) :]
    hidden, width = w2_ref.shape
    per = hidden // width
    quarter = all_ref.shape[1] // 4
    pq = width // 4
    ph, wh = width // 2, hidden // 2
    step = pl.program_id(0)

    def weights(act):
        z, x, core, pair = meta[0], meta[1], meta[2], meta[3]
        xs = meta[4]
        at = 0
        for ref, place in zip(pieces, places):
            for row, rows, kz, kx, ky, kc, part in place:
                shard = (z ^ kz) * xs + (x ^ kx)
                col = ((pair ^ ky) * 2 + (core ^ kc)) * quarter
                copy = pltpu.make_async_copy(
                    ref.at[pl.ds(row, rows), :],
                    all_ref.at[
                        pl.ds(pl.multiple_of(shard * rps + part, rows), rows),
                        pl.ds(pl.multiple_of(col, 128), quarter),
                    ],
                    sems.at[at],
                )
                copy.start() if act == "start" else copy.wait()
                at += 1

    @pl.when(step == 0)
    def _():
        weights("start")
        acc1_ref[...] = jnp.zeros_like(acc1_ref)
        acc2_ref[...] = jnp.zeros_like(acc2_ref)
        accp_ref[...] = jnp.zeros_like(accp_ref)
        vec_ref[...] = jnp.zeros_like(vec_ref)
        weights("wait")
        for r in range(4):
            wp_ref[:, r * pq : (r + 1) * pq] = all_ref[:, r * quarter : r * quarter + pq]
        at = pq + hidden // 4
        for shard in range(width // rps):
            for b in range(per):
                to = (shard * per + b) * rps
                w2_ref[to : to + rps, :] = all_ref[
                    shard * rps : (shard + 1) * rps, b * quarter + at : b * quarter + at + width
                ]

    o, y = o_ref[...], y_ref[...]
    r1 = x_ref[...].astype(F32) + dot(o, wp_ref[...])
    n, rstd = normed(r1)
    gain = vector(slots_ref, 3, nslot)
    h = (n * gain + vector(slots_ref, 4, nslot)).astype(BF)
    ht = h.T
    out = r1 + vector(slots_ref, 0, nslot)
    dh = jnp.zeros_like(r1)
    for j in range(per):
        at = slice(j * width, (j + 1) * width)
        w1 = all_ref[:, j * quarter + pq : j * quarter + pq + width]
        u = dot(h, w1) + vector(slots_ref, 5 + j, nslot)
        da = dot_nt(y, w2_ref[at, :])
        cdf = 0.5 + 0.5 * lax.erf(u * 0.7071067811865476)
        pdf = jnp.exp(u * u * -0.5) * 0.3989422804014327
        a = (u * cdf).astype(BF)
        du = (da * (cdf + u * pdf)).astype(BF)
        out += dot(a, w2_ref[at, :])
        dh += dot_nt(du, w1)
        acc1_ref[:, at] += dot(ht, du)
        acc2_ref[at, :] += dot_tn(a, y)
        vec_ref[0:1, at] += jnp.sum(du.astype(F32), axis=0, keepdims=True)
    out_ref[...] = out
    yf = y.astype(F32)
    dr = yf + norm_back(dh * gain, n, rstd)
    dr_ref[...] = dr
    accp_ref[...] += dot_tn(o, dr.astype(BF))
    vec_ref[1:2, :width] += jnp.sum(yf, axis=0, keepdims=True)
    vec_ref[2:3, :width] += jnp.sum(dh * n, axis=0, keepdims=True)
    vec_ref[3:4, :width] += jnp.sum(dh, axis=0, keepdims=True)

    @pl.when(step == pl.num_programs(0) - 1)
    def _():
        for which, ref in ((0, keep_ref), (1, send_ref)):
            half = meta[2] if which == 0 else 1 - meta[2]
            pcol = pl.ds(pl.multiple_of(half * ph, 128), ph)
            ref[:, :ph] = accp_ref[:, pcol].astype(BF)
            ref[:, ph : ph + wh] = acc1_ref[:, pl.ds(pl.multiple_of(half * wh, 128), wh)].astype(BF)
            for shard in range(width // rps):
                for j in range(per):
                    at = (shard * per + j) * rps
                    ref[shard * rps : (shard + 1) * rps, ph + wh + j * ph : ph + wh + (j + 1) * ph] = (
                        acc2_ref[at : at + rps, pcol].astype(BF)
                    )


def back_kernel(meta, *refs, seqs, span, begin):
    (
        dr_ref,
        x_ref,
        qkv_ref,
        lse_ref,
        w_ref,
        wp_ref,
        slots_ref,
        from_ref,
        pbias_ref,
    ) = refs[:9]
    if begin:
        dqkv_ref, dpool_ref, acc_ref, dkvb_ref = refs[9:]
    else:
        sum_ref, _, _, dqkv_ref, dpool_ref, keep_ref, send_ref, vec_ref, acc_ref, dkvb_ref = refs[9:]
    width = x_ref.shape[1]
    scale = (width // HEADS) ** -0.5
    step = pl.program_id(0)

    @pl.when(step == 0)
    def _():
        acc_ref[...] = jnp.zeros_like(acc_ref) if begin else sum_ref[...]

    nslot = pbias_ref.shape[1]
    cp = -(-nslot // 16) * 16
    gain, shift = vector(slots_ref, 1, nslot), vector(slots_ref, 2, nslot)
    seq0 = (step + (0 if begin else pl.num_programs(0))) * seqs
    pool = jnp.concatenate(
        [pooled_tokens(slots_ref, seq0 + i, nslot, cp) for i in range(seqs)], axis=0
    )
    pooled_h = (pool * gain + shift).astype(BF)
    kvb = dot(pooled_h, w_ref[:, width:]).astype(BF)
    dr = dr_ref[...]
    do = dot_nt(dr.astype(BF), wp_ref[...]).astype(BF)
    pairs = range(HEADS // 2)
    col = lambda part, p: slice(part * width + p * 128, part * width + (p + 1) * 128)
    for s in range(seqs):
        rows = slice(s * span, (s + 1) * span)
        prow = slice(s * cp, (s + 1) * cp)
        bias = span_bias(from_ref[s], padded(pbias_ref[s], cp, masked))
        both = lambda part, p: jnp.concatenate(
            [qkv_ref[rows, col(part, p)], kvb[prow, col(part - 1, p)]], axis=0
        )
        q = [qkv_ref[rows, col(0, p)] for p in pairs]
        g = [do[rows, col(0, p)] for p in pairs]
        keys = [both(1, p) for p in pairs]
        scores = [dot(keys[p], two_heads_lanes(q[p].T)) + bias for p in pairs]
        dprob = [dot(both(2, p), two_heads_lanes(g[p].T)) for p in pairs]
        prob = [jnp.exp(scores[p] - lse_ref[s, p : p + 1, :]) for p in pairs]
        weighted = [prob[p] * dprob[p] for p in pairs]
        ds = [
            (weighted[p] - prob[p] * jnp.sum(weighted[p], axis=0, keepdims=True)).astype(BF)
            for p in pairs
        ]
        dv = [dot(prob[p].astype(BF), two_heads_rows(g[p])).astype(BF) for p in pairs]
        dq = [(diagonal(dot_tn(keys[p], ds[p])) * scale).astype(BF) for p in pairs]
        dk = [dot(ds[p], two_heads_rows(q[p])).astype(BF) for p in pairs]
        for p in pairs:
            dqkv_ref[rows, col(0, p)] = dq[p].T
            dqkv_ref[rows, col(1, p)] = dk[p][:span]
            dqkv_ref[rows, col(2, p)] = dv[p][:span]
            dkvb_ref[prow, col(0, p)] = dk[p][span:]
            dkvb_ref[prow, col(1, p)] = dv[p][span:]
    n, _ = normed(x_ref[...].astype(F32))
    h = (n * gain + shift).astype(BF)
    dqkv, dkvb = dqkv_ref[...], dkvb_ref[...]
    acc_ref[:width] += dot_tn(h, dqkv)
    acc_ref[:width, width:] += dot_tn(pooled_h, dkvb)
    acc_ref[width : width + 1] += jnp.sum(dqkv.astype(F32), axis=0, keepdims=True)
    acc_ref[width : width + 1, width:] += jnp.sum(dkvb.astype(F32), axis=0, keepdims=True)
    dpool_ref[...] = dot_nt(dkvb, w_ref[:, width:]).astype(BF).reshape(seqs, cp, width)
    if begin:
        return

    @pl.when(step == pl.num_programs(0) - 1)
    def _():
        nh = acc_ref.shape[1] // 2
        for which, ref in ((0, keep_ref), (1, send_ref)):
            half = meta[2] if which == 0 else 1 - meta[2]
            ref[...] = acc_ref[:width, pl.ds(pl.multiple_of(half * nh, 128), nh)].astype(BF)
        w = w_ref[...].astype(F32)

        def row(m):
            total = jnp.sum(m, axis=1, keepdims=True)
            return jnp.broadcast_to(total, (width, 128)).T[:1]

        dshift = row(w * acc_ref[width : width + 1])
        dgain = (row(w * acc_ref[:width]) - shift * dshift) / gain
        vec_ref[0:1] = dgain
        vec_ref[1:2] = dshift


def last_kernel(meta, len_ref, dr_ref, x_ref, dqkv_ref, w_ref, dpool_ref, slots_ref, out_ref, *, seqs, span, nslot):
    n, rstd = normed(x_ref[...].astype(F32))
    dh = dot_nt(dqkv_ref[...], w_ref[...])
    for i in range(seqs):
        starts = doc_starts(len_ref, pl.program_id(0) * seqs + i)
        first = first_member(starts, (meta[0] * meta[4] + meta[1]) * span, span)
        rows = slice(i * span, (i + 1) * span)
        count = jnp.full((1, 1), span - first, jnp.int32).astype(F32)
        share = dpool_ref[i] / count
        row = lax.broadcasted_iota(jnp.int32, (span, n.shape[1]), 0)
        e = (dh[rows] + jnp.where(row >= first, share, 0.0)) * vector(slots_ref, 1, nslot)
        out_ref[rows, :] = dr_ref[rows, :] + norm_back(e, n[rows], rstd[rows])


def after(a, *first):
    return lax.optimization_barrier((a, *first))[0]


def params(mib):
    return pltpu.CompilerParams(dimension_semantics=("arbitrary",), vmem_limit_bytes=mib * MIB)


LITTLE = pl.CostEstimate(flops=1, bytes_accessed=1, transcendentals=0)


def local(
    tokens,
    cotangent,
    doc_lengths,
    attend,
    project,
    widen,
    narrow,
    hidden_bias,
    final_bias,
    gain_first,
    shift_first,
    gain_second,
    shift_second,
    *,
    sizes,
):
    zs, xs, ys, cs = sizes
    nshard = zs * xs
    seq_count, span, width = tokens.shape
    rows = seq_count * span
    hidden = widen.shape[1]
    rps = attend.shape[0]
    rep, shard = lax.axis_index("rep"), lax.axis_index("shard")
    z, x, y, core = shard // xs, shard % xs, rep // cs, rep % cs
    meta = jnp.stack([z, x, core, y % 2, jnp.int32(xs)]).astype(jnp.int32)

    def swap(a, z=0, x=0, y=0, c=0):
        perm = []
        for r in range(ys * cs):
            for s in range(nshard):
                r2 = (r // cs ^ y) * cs + (r % cs ^ c)
                s2 = (s // xs ^ z) * xs + (s % xs ^ x)
                perm.append((r * nshard + s, r2 * nshard + s2))
        return lax.ppermute(a, ("rep", "shard"), perm)

    bits = lambda n: [1 << i for i in range(n.bit_length() - 1)]

    def send(a, dz=0, dx=0, dy=0, dc=0):
        perm = []
        for r in range(ys * cs):
            for s in range(nshard):
                r2 = (r // cs + dy) % ys * cs + (r % cs + dc) % cs
                s2 = (s // xs + dz) % zs * xs + (s % xs + dx) % xs
                perm.append((r * nshard + s, r2 * nshard + s2))
        return lax.ppermute(a, ("rep", "shard"), perm)

    def levels(a):
        return jnp.concatenate([a] + [swap(a, z=k) for k in range(1, zs)], axis=0)

    def sides(a):
        return [a] + [swap(a, x=k) for k in range(1, xs)]

    x2 = tokens.reshape(rows, width)
    y2 = cotangent.reshape(rows, width)
    smem = pl.BlockSpec(memory_space=pltpu.SMEM)
    hbm = pl.BlockSpec(memory_space=pl.ANY)
    nh = attend.shape[1] // 2
    per = hidden // width
    hs = hidden_bias.shape[0]
    attend_col = levels(lax.dynamic_slice_in_dim(attend, core * nh, nh, 1))

    small = jnp.stack([final_bias, gain_first, shift_first, gain_second, shift_second])
    total = seq_count + 5 + 4
    pool_seqs = 8
    packed, doc_from, pbias = pl.pallas_call(
        functools.partial(prep_kernel, sizes=(zs, xs), seqs=pool_seqs),
        grid=(seq_count // pool_seqs,),
        in_specs=[
            smem,
            smem,
            pl.BlockSpec((pool_seqs * span, width), lambda i: (i, 0)),
            pl.BlockSpec((5, rps), lambda i: (0, 0)),
            pl.BlockSpec((1, hs), lambda i: (0, 0)),
        ],
        out_specs=[
            pl.BlockSpec((total, width), lambda i: (0, 0)),
            pl.BlockSpec((pool_seqs, 1, span), lambda i: (i, 0, 0)),
            pl.BlockSpec((pool_seqs, nshard, span), lambda i: (i, 0, 0)),
        ],
        out_shape=[
            jax.ShapeDtypeStruct((total, width), F32),
            jax.ShapeDtypeStruct((seq_count, 1, span), jnp.int32),
            jax.ShapeDtypeStruct((seq_count, nshard, span), F32),
        ],
        compiler_params=params(58),
        cost_estimate=LITTLE,
        name="prep",
    )(meta, doc_lengths, x2, small, hidden_bias[None])
    slots = packed
    for b in bits(zs):
        slots = jnp.concatenate([slots, swap(slots, z=b)], axis=0)
    for b in bits(xs):
        slots = jnp.concatenate([slots, swap(slots, x=b)], axis=0)

    ph, wh = width // 2, hidden // 2
    pair = y % 2
    mine = pair * 2 + core
    cut = lambda a, axis: lax.dynamic_slice_in_dim(
        a, mine * (a.shape[axis] // 4), a.shape[axis] // 4, axis
    )
    ffn_own = jnp.concatenate([cut(project, 1), cut(widen, 1), cut(narrow, 0)], axis=1)
    attend_cols = sides(attend_col)
    attend_parts = attend_cols + [swap(m, c=1) for m in attend_cols]
    ffn_col = levels(after(ffn_own, attend_col)).reshape(zs, rps, -1)
    kr = rps // 2
    over_xs = [ffn_col[:, :kr].reshape(zs * kr, -1)]
    for b in bits(xs):
        over_xs.append(swap(jnp.concatenate(over_xs, axis=0), x=b))
    over_ys = [ffn_col[:, kr:].reshape(zs * kr, -1)]
    over_ys.append(swap(over_ys[0], y=1))

    seqs = 4
    calls = 2
    steps = seq_count // seqs // calls
    all_spec = lambda a, b: pl.BlockSpec((a, b), lambda i, m: (0, 0))
    row_spec = lambda n, w, c=0: pl.BlockSpec((n, w), lambda i, m: (i + c * steps, 0))
    seq_spec = lambda n, a, b, c=0: pl.BlockSpec((n, a, b), lambda i, m: (i + c * steps, 0, 0))
    act_specs = lambda c: [
        row_spec(seqs * span, 3 * width, c),
        row_spec(seqs * span, width, c),
        seq_spec(seqs, HEADS // 2, 2 * span, c),
    ]
    act_shapes = [
        jax.ShapeDtypeStruct((rows, 3 * width), BF),
        jax.ShapeDtypeStruct((rows, width), BF),
        jax.ShapeDtypeStruct((seq_count, HEADS // 2, 2 * span), F32),
    ]

    def attention(c, x2, weights, before):
        return pl.pallas_call(
            functools.partial(
                attend_kernel,
                sizes=(zs, xs),
                seqs=seqs,
                span=span,
                rps=rps,
                start=c * steps * seqs,
            ),
            grid_spec=pltpu.PrefetchScalarGridSpec(
                num_scalar_prefetch=1,
                grid=(steps,),
                in_specs=[
                    row_spec(seqs * span, width, c),
                    all_spec(nshard * total, width),
                    seq_spec(seqs, 1, span, c),
                    seq_spec(seqs, nshard, span, c),
                ]
                + ([all_spec(width, 3 * width)] if c else [hbm] * len(weights))
                + [hbm] * len(before),
                out_specs=([] if c else [all_spec(width, 3 * width)]) + act_specs(c),
                scratch_shapes=[] if c else [pltpu.SemaphoreType.DMA((1, 2 * nshard))],
            ),
            out_shape=([] if c else [jax.ShapeDtypeStruct((width, 3 * width), BF)]) + act_shapes,
            input_output_aliases={6 + i: i for i in range(len(before))},
            compiler_params=params(58),
            cost_estimate=LITTLE,
            name="attention",
        )(meta, x2, slots, doc_from, pbias, *weights, *before)

    w_all, qkv, o, lse = attention(0, after(x2, ffn_col), attend_parts, [])
    over_xs, over_ys = after(over_xs, lse), after(over_ys, lse)
    if len(over_xs) > 1:
        over_xs = [jnp.concatenate(over_xs, axis=0)]
    over_ys = [jnp.concatenate(over_ys, axis=0)]
    both = [over_xs[0], over_ys[0]]
    both_other = [swap(a, c=1) for a in both]
    ends = [swap(over_xs[0], y=1)]
    so_far = over_ys
    for b in bits(xs):
        so_far.append(swap(jnp.concatenate(so_far, axis=0), x=b))
    ends += so_far[1:]
    qkv, o, lse = attention(1, after(x2, *both), [w_all], [qkv, o, lse])
    ends = after(ends, lse)
    ffn_parts = both + both_other + ends + [swap(a, c=1) for a in ends]
    two = [[(kx, 0, 0) for kx in range(xs)], [(0, ky, kr) for ky in range(2)]]
    rest = [[(kx, 1, 0) for kx in range(xs)]]
    rest += [[(kx, ky, kr) for kx in range(b, 2 * b) for ky in range(2)] for b in bits(xs)]
    places = [
        [
            ((i * zs + kz) * kr, kr, kz, kx, ky, kc, part)
            for i, (kx, ky, part) in enumerate(units)
            for kz in range(zs)
        ]
        for group in (two, rest)
        for kc in range(2)
        for units in group
    ]

    tile = 512
    packet = ph + wh + per * ph
    steps, cp = 0, -(-nshard // 16) * 16
    block_out, dr, keep_f, send_f, wp_all, vec_f = pl.pallas_call(
        functools.partial(ffn_kernel, rps=rps, places=places, nslot=nshard),
        grid_spec=pltpu.PrefetchScalarGridSpec(
            num_scalar_prefetch=1,
            grid=(rows // tile,),
            in_specs=[
                row_spec(tile, width),
                row_spec(tile, width),
                row_spec(tile, width),
                all_spec(nshard * total, width),
            ]
            + [hbm] * len(ffn_parts),
            out_specs=[
                row_spec(tile, width),
                row_spec(tile, width),
                all_spec(width, packet),
                all_spec(width, packet),
                all_spec(width, width),
                all_spec(8, hidden),
            ],
            scratch_shapes=[
                pltpu.VMEM((width, width + 2 * hidden), BF),
                pltpu.VMEM((hidden, width), BF),
                pltpu.VMEM((width, hidden), F32),
                pltpu.VMEM((hidden, width), F32),
                pltpu.VMEM((width, width), F32),
                pltpu.SemaphoreType.DMA((sum(len(p) for p in places),)),
            ],
        ),
        out_shape=[
            jax.ShapeDtypeStruct((rows, width), F32),
            jax.ShapeDtypeStruct((rows, width), F32),
            jax.ShapeDtypeStruct((width, packet), BF),
            jax.ShapeDtypeStruct((width, packet), BF),
            jax.ShapeDtypeStruct((width, width), BF),
            jax.ShapeDtypeStruct((8, hidden), F32),
        ],
        compiler_params=params(58),
        cost_estimate=LITTLE,
        name="ffn",
    )(meta, o, x2, y2, slots, *ffn_parts)

    def add(parts, kind):
        total = parts[0].astype(F32)
        for p in parts[1:]:
            total = total + p.astype(F32)
        return total.astype(kind)

    def over_x(a):
        piece = lambda dx: lax.dynamic_slice_in_dim(a, (x + dx) % xs, 1, 1)
        return add([send(piece(dx), dx=dx) if dx else piece(0) for dx in range(xs)], BF)

    def over_y(a):
        n = a.shape[-1] // ys
        piece = lambda dy: lax.dynamic_slice_in_dim(a, (y + dy) % ys * n, n, a.ndim - 1)
        return add([send(piece(dy), dy=dy) if dy else piece(0) for dy in range(ys)], BF)

    def over_z(a):
        k = a.shape[0] // zs
        piece = lambda dz: lax.dynamic_slice_in_dim(a, (z + dz) % zs * k, k, 0)
        parts = [send(piece(dz), dz=dz) if dz else piece(0) for dz in range(zs)]
        return add(parts, BF)

    def over_xy(part):
        n = part.shape[1] // ys
        k = part.shape[0] // nshard
        view = part.reshape(zs, xs, k, ys * n)

        def corner(dx, dy):
            at = (0, (x + dx) % xs, 0, (y + dy) % ys * n)
            return lax.dynamic_slice(view, at, (zs, 1, k, n)).reshape(zs * k, n)

        parts = [
            send(corner(dx, dy), dx=dx, dy=dy) if dx or dy else corner(0, 0)
            for dx in range(xs)
            for dy in range(ys)
        ]
        return add(parts, BF)

    def replicas(part):
        found = {
            (dy, dc): send(part, dy=dy, dc=dc) if dy or dc else part
            for dy in range(ys)
            for dc in range(cs)
        }
        total = []
        for at in range(ys * cs):
            picked = jnp.zeros(part.shape, F32)
            for (dy, dc), piece in found.items():
                mine = ((y - dy + ys) % ys == at % ys) & ((core - dc + cs) % cs == at // ys)
                picked = jnp.where(mine, piece.astype(F32), picked)
            total.append(picked)
        return total

    steps = seq_count // seqs // calls

    def back(c, dr, before):
        nacc = width + 8
        sums = [all_spec(nacc, 3 * width)]
        halves = [all_spec(width, 3 * width // 2)] * 2 + [all_spec(8, width)]
        half_shapes = [
            jax.ShapeDtypeStruct((width, 3 * width // 2), BF),
            jax.ShapeDtypeStruct((width, 3 * width // 2), BF),
            jax.ShapeDtypeStruct((8, width), F32),
        ]
        return pl.pallas_call(
            functools.partial(back_kernel, seqs=seqs, span=span, begin=c == 0),
            grid_spec=pltpu.PrefetchScalarGridSpec(
                num_scalar_prefetch=1,
                grid=(steps,),
                in_specs=[
                    row_spec(seqs * span, width, c),
                    row_spec(seqs * span, width, c),
                    row_spec(seqs * span, 3 * width, c),
                    seq_spec(seqs, HEADS // 2, 2 * span, c),
                    all_spec(width, 3 * width),
                    all_spec(width, width),
                    all_spec(nshard * total, width),
                    seq_spec(seqs, 1, span, c),
                    seq_spec(seqs, nshard, span, c),
                ]
                + ((sums + [hbm, hbm]) if c else []),
                out_specs=[row_spec(seqs * span, 3 * width, c), seq_spec(seqs, cp, width, c)]
                + (halves if c else sums),
                scratch_shapes=([pltpu.VMEM((nacc, 3 * width), F32)] if c else [])
                + [pltpu.VMEM((seqs * cp, 2 * width), BF)],
            ),
            out_shape=[
                jax.ShapeDtypeStruct((rows, 3 * width), BF),
                jax.ShapeDtypeStruct((seq_count, cp, width), BF),
            ]
            + (half_shapes if c else [jax.ShapeDtypeStruct((nacc, 3 * width), F32)]),
            input_output_aliases={11: 0, 12: 1} if c else {},
            compiler_params=params(58),
            cost_estimate=LITTLE,
            name="back",
        )(meta, dr, x2, qkv, lse, w_all, wp_all, slots, doc_from, pbias, *before)

    dqkv, dpool, sums = back(0, dr, [])
    part_f = add([keep_f, after(send(send_f, dc=1), sums)], BF)
    dqkv, dpool, keep_a, send_a, vec_a = back(1, after(dr, part_f), [sums, dqkv, dpool])
    kf = part_f.shape[0] // nshard
    view = part_f.reshape(zs, xs, kf, packet)
    first_f = over_x(view[:, :, : kf // 2])
    second_f = over_y(view[:, :, kf // 2 :])

    dpool, keep_a = after((dpool, keep_a), first_f, second_f)
    part_a = add([keep_a, send(send_a, dc=1)], BF)
    part_f = jnp.concatenate([over_y(first_f), over_x(second_f)], axis=2)
    part_f = part_f.reshape(zs * kf, packet // ys)
    share_a = over_xy(part_a)
    share_f = over_z(part_f)
    grad_f = jnp.concatenate(replicas(share_f), axis=1)
    halves = [grad_f[:, i * packet : (i + 1) * packet] for i in range(2)]
    grad_project = jnp.concatenate([h[:, :ph] for h in halves], axis=1)
    grad_widen = jnp.concatenate([h[:, ph : ph + wh] for h in halves], axis=1)
    grad_narrow = jnp.concatenate(
        [
            jnp.concatenate(
                [h[:, ph + wh + j * ph : ph + wh + (j + 1) * ph] for h in halves], axis=1
            )
            for j in range(per)
        ],
        axis=0,
    )

    vec = jnp.concatenate(
        [vec_f[0].reshape(per, width), vec_f[1:2, :width], vec_a[:2], vec_f[2:4, :width]], axis=0
    ).astype(BF)
    nvec = vec.shape[0]
    dp = jnp.transpose(dpool[:, :nshard], (1, 0, 2)).reshape(xs, zs, seq_count, width)
    dp = jnp.concatenate([dp, jnp.broadcast_to(vec, (xs, zs, nvec, width))], axis=2)
    for b in reversed(bits(xs)):
        dp = add([dp[:b], swap(dp[b:], x=b)], BF)
    dp = dp[0]
    for b in reversed(bits(zs)):
        dp = add([dp[:b], swap(dp[b:], z=b)], BF)
    own = dp[0].astype(F32)
    own_vec = jnp.concatenate(
        [lax.dynamic_slice(own[seq_count:].reshape(nvec * width), (shard * hs,), (hs,))]
        + [
            lax.dynamic_slice(own[seq_count + per + i], (shard * rps,), (rps,))
            for i in range(5)
        ]
    ).astype(BF)
    tokens_grad = pl.pallas_call(
        functools.partial(last_kernel, seqs=seqs, span=span, nslot=nshard),
        grid=(seq_count // seqs,),
        in_specs=[
            smem,
            smem,
            pl.BlockSpec((seqs * span, width), lambda i: (i, 0)),
            pl.BlockSpec((seqs * span, width), lambda i: (i, 0)),
            pl.BlockSpec((seqs * span, 3 * width), lambda i: (i, 0)),
            pl.BlockSpec((width, 3 * width), lambda i: (0, 0)),
            pl.BlockSpec((seqs, 1, width), lambda i: (i, 0, 0)),
            pl.BlockSpec((nshard * total, width), lambda i: (0, 0)),
        ],
        out_specs=pl.BlockSpec((seqs * span, width), lambda i: (i, 0)),
        out_shape=jax.ShapeDtypeStruct((rows, width), F32),
        compiler_params=params(58),
        cost_estimate=LITTLE,
        name="last",
    )(
        meta,
        doc_lengths,
        after(dr, part_a),
        x2,
        dqkv,
        w_all,
        own[:seq_count].reshape(seq_count, 1, width),
        slots,
    )

    share_a = over_z(share_a)
    ncol = share_a.shape[1]
    vrows = -(-own_vec.shape[0] // ncol)
    own_vec = jnp.pad(own_vec, (0, vrows * ncol - own_vec.shape[0])).reshape(vrows, ncol)
    found = replicas(jnp.concatenate([share_a, own_vec], axis=0))
    grad_attend = jnp.concatenate([f[:rps] for f in found], axis=1)
    vec = sum(f[rps:] for f in found).reshape(vrows * ncol)
    vecs = [vec[:hs]] + [vec[hs + i * rps : hs + (i + 1) * rps] for i in range(5)]
    return (
        block_out.reshape(tokens.shape),
        tokens_grad.reshape(tokens.shape),
        grad_attend,
        grad_project,
        grad_widen,
        grad_narrow,
        *vecs,
    )


def solution(mesh):
    first = mesh.devices[0]
    xs = len({d.coords[0] for d in first})
    cs = len({d.core_on_chip for d in mesh.devices[:, 0]})
    sizes = (mesh.shape["shard"] // xs, xs, mesh.shape["rep"] // cs, cs)
    row = P("shard", None)
    vec = P("shard")
    act = P("rep", "shard", None)
    return jax.shard_map(
        functools.partial(local, sizes=sizes),
        mesh=mesh,
        in_specs=(act, act, P("rep", None), row, row, row, row) + (vec,) * 6,
        out_specs=(act, act, row, row, row, row) + (vec,) * 6,
        check_vma=False,
    )
```

```python
import functools

import jax
import jax.numpy as jnp
from jax import lax
from jax.experimental import pallas as pl
from jax.experimental.pallas import tpu as pltpu
from jax.sharding import PartitionSpec as P

HEADS = 8
epsilon = 1e-05
masked = -1e30
F32 = jnp.float32
BF = jnp.bfloat16
MIB = 1 << 20


def dot(a, b):
    return jnp.dot(a, b, preferred_element_type=F32)


def dot_nt(a, b):
    return lax.dot_general(a, b, (((1,), (1,)), ((), ())), preferred_element_type=F32)


def dot_tn(a, b):
    return lax.dot_general(a, b, (((0,), (0,)), ((), ())), preferred_element_type=F32)


def normed(v):
    center = v - jnp.mean(v, axis=-1, keepdims=True)
    rstd = lax.rsqrt(jnp.mean(center * center, axis=-1, keepdims=True) + epsilon)
    return center * rstd, rstd


def norm_back(e, n, rstd):
    return rstd * (
        e - jnp.mean(e, axis=-1, keepdims=True) - n * jnp.mean(e * n, axis=-1, keepdims=True)
    )


def two_heads_lanes(t):
    half = t.shape[0] // 2
    zero = jnp.zeros((half, t.shape[1]), t.dtype)
    left = jnp.concatenate([t[:half], zero], axis=0)
    right = jnp.concatenate([zero, t[half:]], axis=0)
    return jnp.concatenate([left, right], axis=1)


def two_heads_rows(a):
    first = lax.broadcasted_iota(jnp.int32, a.shape, 1) < a.shape[1] // 2
    zero = jnp.zeros_like(a)
    return jnp.concatenate([jnp.where(first, a, zero), jnp.where(first, zero, a)], axis=0)


def diagonal(t):
    rows, cols = t.shape[0] // 2, t.shape[1] // 2
    return jnp.concatenate([t[:rows, :cols], t[rows:, cols:]], axis=0)


def span_bias(doc_from, pooled):
    span = doc_from.shape[1]
    key = lax.broadcasted_iota(jnp.int32, (span, span), 0)
    query = lax.broadcasted_iota(jnp.int32, (span, span), 1)
    direct = jnp.where((key >= doc_from) & (key <= query), 0.0, masked).astype(F32)
    both = jnp.concatenate([direct, pooled], axis=0)
    return jnp.concatenate([both, both], axis=1)


def arriving(meta, sizes, pieces, places, sems, act, kind):
    zs, xs = sizes
    z, x, core = meta[0], meta[1], meta[2]
    at = 0
    for which in range(2):
        half = core if which == 0 else 1 - core
        for kx in range(xs):
            for kz in range(zs):
                shard = (z ^ kz) * xs + (x ^ kx)
                for src, dst in places[kind](pieces, which, kx, kz, shard, half):
                    copy = pltpu.make_async_copy(src, dst, sems.at[kind, at])
                    copy.start() if act == "start" else copy.wait()
                    at += 1


def doc_starts(len_ref, seq):
    starts = [jnp.int32(0)]
    for j in range(len_ref.shape[1] - 1):
        starts.append(starts[-1] + len_ref[seq, j])
    return starts


def start_at(starts, position):
    found = jnp.zeros_like(position)
    for start in starts:
        found = jnp.where(position >= start, start, found)
    return found


def first_member(starts, base, span):
    return jnp.maximum(start_at(starts, base + span - 1) - base, 0)


def prep_kernel(meta, len_ref, x_ref, small_ref, hidden_ref, out_ref, from_ref, pbias_ref, *, sizes, seqs):
    zs, xs = sizes
    z, x = meta[0], meta[1]
    shard = z * xs + x
    nshard, span = pbias_ref.shape[1:]
    width = x_ref.shape[1]
    total = out_ref.shape[0] - small_ref.shape[0] - 4
    step = pl.program_id(0)
    base = shard * span

    @pl.when(step == 0)
    def _():
        def place(v, at):
            row = lax.broadcasted_iota(jnp.int32, (v.shape[1], width), 0)
            lane = lax.broadcasted_iota(jnp.int32, (v.shape[1], width), 1)
            return dot(v, (lane == row + at).astype(F32).astype(BF))

        nsmall, n = small_ref.shape
        rows = [place(small_ref[...], shard * n)]
        for r in range(4):
            rows.append(place(hidden_ref[...], shard * hidden_ref.shape[1] - r * width))
        out_ref[total:, :] = jnp.concatenate(rows, axis=0)

    n, _ = normed(x_ref[...].astype(F32))
    row = lax.broadcasted_iota(jnp.int32, (span, width), 0)
    slot = lax.broadcasted_iota(jnp.int32, (nshard, span), 0)
    slot_span = (z ^ (slot & (zs - 1))) * xs + (x ^ (slot // zs))
    slot_last = slot_span * span + span - 1
    position = base + lax.broadcasted_iota(jnp.int32, (1, span), 1)
    pooled = []
    for i in range(seqs):
        starts = doc_starts(len_ref, step * seqs + i)
        first = first_member(starts, base, span)
        part = jnp.where(row >= first, n[i * span : (i + 1) * span], 0.0)
        count = jnp.full((1, 1), span - first, jnp.int32).astype(F32)
        pooled.append(jnp.sum(part, axis=0, keepdims=True) / count)
        here = start_at(starts, position)
        from_ref[i] = here - base
        last = start_at(starts, slot_last)
        counts = jnp.minimum(span, slot_last + 1 - last).astype(F32)
        seen = (slot_span < shard) & (last == here)
        pbias_ref[i] = jnp.where(seen, jnp.log(counts), masked)
    at = pl.multiple_of(step * seqs, seqs)
    out_ref[pl.ds(at, seqs), :] = jnp.concatenate(pooled, axis=0)


def padded(a, rows, value):
    shape = a.shape[:-2] + (rows - a.shape[-2], a.shape[-1])
    return jnp.concatenate([a, jnp.full(shape, value, a.dtype)], axis=-2) if shape[-2] else a


def vector(slots_ref, i, nslot):
    total = slots_ref.shape[0] // nslot
    at = [k * total + total - 9 + i for k in range(nslot)]
    return sum(slots_ref[k : k + 1, :] for k in at)


def pooled_tokens(slots_ref, seq, nslot, cp):
    total = slots_ref.shape[0] // nslot
    rows = [slots_ref[pl.ds(k * total + seq, 1), :] for k in range(nslot)]
    return padded(jnp.concatenate(rows, axis=0), cp, 0.0)


def attend_kernel(meta, *refs, sizes, seqs, span, rps, start):
    x_ref, slots_ref, from_ref, pbias_ref = refs[:4]
    width = x_ref.shape[1]
    nslot = pbias_ref.shape[1]
    cp = -(-nslot // 16) * 16
    gain, shift = vector(slots_ref, 1, nslot), vector(slots_ref, 2, nslot)
    seq0 = pl.program_id(0) * seqs + start
    if start:
        w_ref, _, _, _, qkv_ref, o_ref, lse_ref = refs[4:]
    else:
        xs = sizes[1]
        pieces = refs[4 : 4 + 2 * xs]
        w_ref, qkv_ref, o_ref, lse_ref, sems = refs[4 + 2 * xs :]
        nh = w_ref.shape[1] // 2

        def place(pieces, which, kx, kz, shard, half):
            yield (
                pieces[which * xs + kx].at[pl.ds(kz * rps, rps), :],
                w_ref.at[
                    pl.ds(pl.multiple_of(shard * rps, rps), rps),
                    pl.ds(pl.multiple_of(half * nh, 128), nh),
                ],
            )

        @pl.when(pl.program_id(0) == 0)
        def _():
            arriving(meta, sizes, pieces, [place], sems, "start", 0)

    n, _ = normed(x_ref[...].astype(F32))
    h = (n * gain + shift).astype(BF)
    pooled_h = jnp.concatenate(
        [pooled_tokens(slots_ref, seq0 + i, nslot, cp) for i in range(seqs)], axis=0
    )
    pooled_h = pooled_h * gain + shift
    if not start:

        @pl.when(pl.program_id(0) == 0)
        def _():
            arriving(meta, sizes, pieces, [place], sems, "wait", 0)

    qkv = dot(h, w_ref[...]).astype(BF)
    q = qkv[:, :width] * jnp.asarray((width // HEADS) ** -0.5, BF)
    qkv_ref[:, :width] = q
    qkv_ref[:, width:] = qkv[:, width:]
    kvb = dot(pooled_h.astype(BF), w_ref[:, width:]).astype(BF)
    pairs = range(HEADS // 2)
    col = lambda part, p: slice(part * width + p * 128, part * width + (p + 1) * 128)
    for s in range(seqs):
        rows = slice(s * span, (s + 1) * span)
        prow = slice(s * cp, (s + 1) * cp)
        bias = span_bias(from_ref[s], padded(pbias_ref[s], cp, masked))
        both = lambda part, p: jnp.concatenate(
            [qkv[rows, col(part, p)], kvb[prow, col(part - 1, p)]], axis=0
        )
        query = [two_heads_lanes(q[rows, col(0, p)].T) for p in pairs]
        scores = [dot(both(1, p), query[p]) + bias for p in pairs]
        top = [jnp.max(scores[p], axis=0, keepdims=True) for p in pairs]
        e = [jnp.exp(scores[p] - top[p]) for p in pairs]
        total = [jnp.sum(e[p], axis=0, keepdims=True) for p in pairs]
        prob = [(e[p] * (1.0 / total[p])).astype(BF) for p in pairs]
        out = [diagonal(dot_tn(both(2, p), prob[p])).astype(BF) for p in pairs]
        for p in pairs:
            lse_ref[s, p : p + 1, :] = top[p] + jnp.log(total[p])
            o_ref[rows, col(0, p)] = out[p].T


def ffn_kernel(meta, *refs, rps, places, nslot):
    o_ref, x_ref, y_ref, slots_ref = refs[:4]
    pieces = refs[4 : 4 + len(places)]
    (
        out_ref,
        dr_ref,
        keep_ref,
        send_ref,
        wp_ref,
        vec_ref,
        all_ref,
        w2_ref,
        acc1_ref,
        acc2_ref,
        accp_ref,
        sems,
    ) = refs[4 + len(places) :]
    hidden, width = w2_ref.shape
    per = hidden // width
    quarter = all_ref.shape[1] // 4
    pq = width // 4
    ph, wh = width // 2, hidden // 2
    step = pl.program_id(0)

    def weights(act):
        z, x, core, pair = meta[0], meta[1], meta[2], meta[3]
        xs = meta[4]
        at = 0
        for ref, place in zip(pieces, places):
            for row, rows, kz, kx, ky, kc, part in place:
                shard = (z ^ kz) * xs + (x ^ kx)
                col = ((pair ^ ky) * 2 + (core ^ kc)) * quarter
                copy = pltpu.make_async_copy(
                    ref.at[pl.ds(row, rows), :],
                    all_ref.at[
                        pl.ds(pl.multiple_of(shard * rps + part, rows), rows),
                        pl.ds(pl.multiple_of(col, 128), quarter),
                    ],
                    sems.at[at],
                )
                copy.start() if act == "start" else copy.wait()
                at += 1

    @pl.when(step == 0)
    def _():
        weights("start")
        acc1_ref[...] = jnp.zeros_like(acc1_ref)
        acc2_ref[...] = jnp.zeros_like(acc2_ref)
        accp_ref[...] = jnp.zeros_like(accp_ref)
        vec_ref[...] = jnp.zeros_like(vec_ref)
        weights("wait")
        for r in range(4):
            wp_ref[:, r * pq : (r + 1) * pq] = all_ref[:, r * quarter : r * quarter + pq]
        at = pq + hidden // 4
        for shard in range(width // rps):
            for b in range(per):
                to = (shard * per + b) * rps
                w2_ref[to : to + rps, :] = all_ref[
                    shard * rps : (shard + 1) * rps, b * quarter + at : b * quarter + at + width
                ]

    o, y = o_ref[...], y_ref[...]
    r1 = x_ref[...].astype(F32) + dot(o, wp_ref[...])
    n, rstd = normed(r1)
    gain = vector(slots_ref, 3, nslot)
    h = (n * gain + vector(slots_ref, 4, nslot)).astype(BF)
    ht = h.T
    out = r1 + vector(slots_ref, 0, nslot)
    dh = jnp.zeros_like(r1)
    for j in range(per):
        at = slice(j * width, (j + 1) * width)
        w1 = all_ref[:, j * quarter + pq : j * quarter + pq + width]
        u = dot(h, w1) + vector(slots_ref, 5 + j, nslot)
        da = dot_nt(y, w2_ref[at, :])
        cdf = 0.5 + 0.5 * lax.erf(u * 0.7071067811865476)
        pdf = jnp.exp(u * u * -0.5) * 0.3989422804014327
        a = (u * cdf).astype(BF)
        du = (da * (cdf + u * pdf)).astype(BF)
        out += dot(a, w2_ref[at, :])
        dh += dot_nt(du, w1)
        acc1_ref[:, at] += dot(ht, du)
        acc2_ref[at, :] += dot_tn(a, y)
        vec_ref[0:1, at] += jnp.sum(du.astype(F32), axis=0, keepdims=True)
    out_ref[...] = out
    yf = y.astype(F32)
    dr = yf + norm_back(dh * gain, n, rstd)
    dr_ref[...] = dr
    accp_ref[...] += dot_tn(o, dr.astype(BF))
    vec_ref[1:2, :width] += jnp.sum(yf, axis=0, keepdims=True)
    vec_ref[2:3, :width] += jnp.sum(dh * n, axis=0, keepdims=True)
    vec_ref[3:4, :width] += jnp.sum(dh, axis=0, keepdims=True)

    @pl.when(step == pl.num_programs(0) - 1)
    def _():
        for which, ref in ((0, keep_ref), (1, send_ref)):
            half = meta[2] if which == 0 else 1 - meta[2]
            pcol = pl.ds(pl.multiple_of(half * ph, 128), ph)
            ref[:, :ph] = accp_ref[:, pcol].astype(BF)
            ref[:, ph : ph + wh] = acc1_ref[:, pl.ds(pl.multiple_of(half * wh, 128), wh)].astype(BF)
            for shard in range(width // rps):
                for j in range(per):
                    at = (shard * per + j) * rps
                    ref[shard * rps : (shard + 1) * rps, ph + wh + j * ph : ph + wh + (j + 1) * ph] = (
                        acc2_ref[at : at + rps, pcol].astype(BF)
                    )


def back_kernel(meta, *refs, seqs, span, begin):
    (
        dr_ref,
        x_ref,
        qkv_ref,
        lse_ref,
        w_ref,
        wp_ref,
        slots_ref,
        from_ref,
        pbias_ref,
    ) = refs[:9]
    if begin:
        dqkv_ref, dpool_ref, acc_ref, dkvb_ref = refs[9:]
    else:
        sum_ref, _, _, dqkv_ref, dpool_ref, keep_ref, send_ref, vec_ref, acc_ref, dkvb_ref = refs[9:]
    width = x_ref.shape[1]
    scale = (width // HEADS) ** -0.5
    step = pl.program_id(0)

    @pl.when(step == 0)
    def _():
        acc_ref[...] = jnp.zeros_like(acc_ref) if begin else sum_ref[...]

    nslot = pbias_ref.shape[1]
    cp = -(-nslot // 16) * 16
    gain, shift = vector(slots_ref, 1, nslot), vector(slots_ref, 2, nslot)
    seq0 = (step + (0 if begin else pl.num_programs(0))) * seqs
    pool = jnp.concatenate(
        [pooled_tokens(slots_ref, seq0 + i, nslot, cp) for i in range(seqs)], axis=0
    )
    pooled_h = (pool * gain + shift).astype(BF)
    kvb = dot(pooled_h, w_ref[:, width:]).astype(BF)
    dr = dr_ref[...]
    do = dot_nt(dr.astype(BF), wp_ref[...]).astype(BF)
    pairs = range(HEADS // 2)
    col = lambda part, p: slice(part * width + p * 128, part * width + (p + 1) * 128)
    for s in range(seqs):
        rows = slice(s * span, (s + 1) * span)
        prow = slice(s * cp, (s + 1) * cp)
        bias = span_bias(from_ref[s], padded(pbias_ref[s], cp, masked))
        both = lambda part, p: jnp.concatenate(
            [qkv_ref[rows, col(part, p)], kvb[prow, col(part - 1, p)]], axis=0
        )
        q = [qkv_ref[rows, col(0, p)] for p in pairs]
        g = [do[rows, col(0, p)] for p in pairs]
        keys = [both(1, p) for p in pairs]
        scores = [dot(keys[p], two_heads_lanes(q[p].T)) + bias for p in pairs]
        dprob = [dot(both(2, p), two_heads_lanes(g[p].T)) for p in pairs]
        prob = [jnp.exp(scores[p] - lse_ref[s, p : p + 1, :]) for p in pairs]
        weighted = [prob[p] * dprob[p] for p in pairs]
        ds = [
            (weighted[p] - prob[p] * jnp.sum(weighted[p], axis=0, keepdims=True)).astype(BF)
            for p in pairs
        ]
        dv = [dot(prob[p].astype(BF), two_heads_rows(g[p])).astype(BF) for p in pairs]
        dq = [(diagonal(dot_tn(keys[p], ds[p])) * scale).astype(BF) for p in pairs]
        dk = [dot(ds[p], two_heads_rows(q[p])).astype(BF) for p in pairs]
        for p in pairs:
            dqkv_ref[rows, col(0, p)] = dq[p].T
            dqkv_ref[rows, col(1, p)] = dk[p][:span]
            dqkv_ref[rows, col(2, p)] = dv[p][:span]
            dkvb_ref[prow, col(0, p)] = dk[p][span:]
            dkvb_ref[prow, col(1, p)] = dv[p][span:]
    n, _ = normed(x_ref[...].astype(F32))
    h = (n * gain + shift).astype(BF)
    dqkv, dkvb = dqkv_ref[...], dkvb_ref[...]
    acc_ref[:width] += dot_tn(h, dqkv)
    acc_ref[:width, width:] += dot_tn(pooled_h, dkvb)
    acc_ref[width : width + 1] += jnp.sum(dqkv.astype(F32), axis=0, keepdims=True)
    acc_ref[width : width + 1, width:] += jnp.sum(dkvb.astype(F32), axis=0, keepdims=True)
    dpool_ref[...] = dot_nt(dkvb, w_ref[:, width:]).astype(BF).reshape(seqs, cp, width)
    if begin:
        return

    @pl.when(step == pl.num_programs(0) - 1)
    def _():
        nh = acc_ref.shape[1] // 2
        for which, ref in ((0, keep_ref), (1, send_ref)):
            half = meta[2] if which == 0 else 1 - meta[2]
            ref[...] = acc_ref[:width, pl.ds(pl.multiple_of(half * nh, 128), nh)].astype(BF)
        w = w_ref[...].astype(F32)

        def row(m):
            total = jnp.sum(m, axis=1, keepdims=True)
            return jnp.broadcast_to(total, (width, 128)).T[:1]

        dshift = row(w * acc_ref[width : width + 1])
        dgain = (row(w * acc_ref[:width]) - shift * dshift) / gain
        vec_ref[0:1] = dgain
        vec_ref[1:2] = dshift


def last_kernel(meta, len_ref, dr_ref, x_ref, dqkv_ref, w_ref, dpool_ref, slots_ref, out_ref, *, seqs, span, nslot):
    n, rstd = normed(x_ref[...].astype(F32))
    dh = dot_nt(dqkv_ref[...], w_ref[...])
    for i in range(seqs):
        starts = doc_starts(len_ref, pl.program_id(0) * seqs + i)
        first = first_member(starts, (meta[0] * meta[4] + meta[1]) * span, span)
        rows = slice(i * span, (i + 1) * span)
        count = jnp.full((1, 1), span - first, jnp.int32).astype(F32)
        share = dpool_ref[i] / count
        row = lax.broadcasted_iota(jnp.int32, (span, n.shape[1]), 0)
        e = (dh[rows] + jnp.where(row >= first, share, 0.0)) * vector(slots_ref, 1, nslot)
        out_ref[rows, :] = dr_ref[rows, :] + norm_back(e, n[rows], rstd[rows])


def after(a, *first):
    return lax.optimization_barrier((a, *first))[0]


def params(mib):
    return pltpu.CompilerParams(dimension_semantics=("arbitrary",), vmem_limit_bytes=mib * MIB)


LITTLE = pl.CostEstimate(flops=1, bytes_accessed=1, transcendentals=0)


def local(
    tokens,
    cotangent,
    doc_lengths,
    attend,
    project,
    widen,
    narrow,
    hidden_bias,
    final_bias,
    gain_first,
    shift_first,
    gain_second,
    shift_second,
    *,
    sizes,
):
    zs, xs, ys, cs = sizes
    nshard = zs * xs
    seq_count, span, width = tokens.shape
    rows = seq_count * span
    hidden = widen.shape[1]
    rps = attend.shape[0]
    rep, shard = lax.axis_index("rep"), lax.axis_index("shard")
    z, x, y, core = shard // xs, shard % xs, rep // cs, rep % cs
    meta = jnp.stack([z, x, core, y % 2, jnp.int32(xs)]).astype(jnp.int32)

    def swap(a, z=0, x=0, y=0, c=0):
        perm = []
        for r in range(ys * cs):
            for s in range(nshard):
                r2 = (r // cs ^ y) * cs + (r % cs ^ c)
                s2 = (s // xs ^ z) * xs + (s % xs ^ x)
                perm.append((r * nshard + s, r2 * nshard + s2))
        return lax.ppermute(a, ("rep", "shard"), perm)

    bits = lambda n: [1 << i for i in range(n.bit_length() - 1)]

    def send(a, dz=0, dx=0, dy=0, dc=0):
        perm = []
        for r in range(ys * cs):
            for s in range(nshard):
                r2 = (r // cs + dy) % ys * cs + (r % cs + dc) % cs
                s2 = (s // xs + dz) % zs * xs + (s % xs + dx) % xs
                perm.append((r * nshard + s, r2 * nshard + s2))
        return lax.ppermute(a, ("rep", "shard"), perm)

    def levels(a):
        return jnp.concatenate([a] + [swap(a, z=k) for k in range(1, zs)], axis=0)

    def sides(a):
        return [a] + [swap(a, x=k) for k in range(1, xs)]

    x2 = tokens.reshape(rows, width)
    y2 = cotangent.reshape(rows, width)
    smem = pl.BlockSpec(memory_space=pltpu.SMEM)
    hbm = pl.BlockSpec(memory_space=pl.ANY)
    nh = attend.shape[1] // 2
    per = hidden // width
    hs = hidden_bias.shape[0]
    attend_col = levels(lax.dynamic_slice_in_dim(attend, core * nh, nh, 1))

    small = jnp.stack([final_bias, gain_first, shift_first, gain_second, shift_second])
    total = seq_count + 5 + 4
    pool_seqs = 8
    packed, doc_from, pbias = pl.pallas_call(
        functools.partial(prep_kernel, sizes=(zs, xs), seqs=pool_seqs),
        grid=(seq_count // pool_seqs,),
        in_specs=[
            smem,
            smem,
            pl.BlockSpec((pool_seqs * span, width), lambda i: (i, 0)),
            pl.BlockSpec((5, rps), lambda i: (0, 0)),
            pl.BlockSpec((1, hs), lambda i: (0, 0)),
        ],
        out_specs=[
            pl.BlockSpec((total, width), lambda i: (0, 0)),
            pl.BlockSpec((pool_seqs, 1, span), lambda i: (i, 0, 0)),
            pl.BlockSpec((pool_seqs, nshard, span), lambda i: (i, 0, 0)),
        ],
        out_shape=[
            jax.ShapeDtypeStruct((total, width), F32),
            jax.ShapeDtypeStruct((seq_count, 1, span), jnp.int32),
            jax.ShapeDtypeStruct((seq_count, nshard, span), F32),
        ],
        compiler_params=params(58),
        cost_estimate=LITTLE,
        name="prep",
    )(meta, doc_lengths, x2, small, hidden_bias[None])
    slots = packed
    for b in bits(zs):
        slots = jnp.concatenate([slots, swap(slots, z=b)], axis=0)
    for b in bits(xs):
        slots = jnp.concatenate([slots, swap(slots, x=b)], axis=0)

    ph, wh = width // 2, hidden // 2
    pair = y % 2
    mine = pair * 2 + core
    cut = lambda a, axis: lax.dynamic_slice_in_dim(
        a, mine * (a.shape[axis] // 4), a.shape[axis] // 4, axis
    )
    ffn_own = jnp.concatenate([cut(project, 1), cut(widen, 1), cut(narrow, 0)], axis=1)
    attend_cols = sides(attend_col)
    attend_parts = attend_cols + [swap(m, c=1) for m in attend_cols]
    ffn_col = levels(after(ffn_own, attend_col)).reshape(zs, rps, -1)
    kr = rps // 2
    over_xs = [ffn_col[:, :kr].reshape(zs * kr, -1)]
    for b in bits(xs):
        over_xs.append(swap(jnp.concatenate(over_xs, axis=0), x=b))
    over_ys = [ffn_col[:, kr:].reshape(zs * kr, -1)]
    over_ys.append(swap(over_ys[0], y=1))

    seqs = 4
    calls = 2
    steps = seq_count // seqs // 4
    all_spec = lambda a, b: pl.BlockSpec((a, b), lambda i, m: (0, 0))
    row_spec = lambda n, w, c=0: pl.BlockSpec((n, w), lambda i, m: (i + c * steps, 0))
    seq_spec = lambda n, a, b, c=0: pl.BlockSpec((n, a, b), lambda i, m: (i + c * steps, 0, 0))
    act_specs = lambda c: [
        row_spec(seqs * span, 3 * width, c),
        row_spec(seqs * span, width, c),
        seq_spec(seqs, HEADS // 2, 2 * span, c),
    ]
    act_shapes = [
        jax.ShapeDtypeStruct((rows, 3 * width), BF),
        jax.ShapeDtypeStruct((rows, width), BF),
        jax.ShapeDtypeStruct((seq_count, HEADS // 2, 2 * span), F32),
    ]

    def attention(c, x2, weights, before):
        return pl.pallas_call(
            functools.partial(
                attend_kernel,
                sizes=(zs, xs),
                seqs=seqs,
                span=span,
                rps=rps,
                start=c * steps * seqs,
            ),
            grid_spec=pltpu.PrefetchScalarGridSpec(
                num_scalar_prefetch=1,
                grid=(seq_count // seqs - steps if c else steps,),
                in_specs=[
                    row_spec(seqs * span, width, c),
                    all_spec(nshard * total, width),
                    seq_spec(seqs, 1, span, c),
                    seq_spec(seqs, nshard, span, c),
                ]
                + ([all_spec(width, 3 * width)] if c else [hbm] * len(weights))
                + [hbm] * len(before),
                out_specs=([] if c else [all_spec(width, 3 * width)]) + act_specs(c),
                scratch_shapes=[] if c else [pltpu.SemaphoreType.DMA((1, 2 * nshard))],
            ),
            out_shape=([] if c else [jax.ShapeDtypeStruct((width, 3 * width), BF)]) + act_shapes,
            input_output_aliases={6 + i: i for i in range(len(before))},
            compiler_params=params(58),
            cost_estimate=LITTLE,
            name="attention",
        )(meta, x2, slots, doc_from, pbias, *weights, *before)

    w_all, qkv, o, lse = attention(0, after(x2, ffn_col), attend_parts, [])
    over_xs, over_ys = after(over_xs, lse), after(over_ys, lse)
    if len(over_xs) > 1:
        over_xs = [jnp.concatenate(over_xs, axis=0)]
    over_ys = [jnp.concatenate(over_ys, axis=0)]
    both = [over_xs[0], over_ys[0]]
    both_other = [swap(a, c=1) for a in both]
    ends = [swap(over_xs[0], y=1)]
    so_far = over_ys
    for b in bits(xs):
        so_far.append(swap(jnp.concatenate(so_far, axis=0), x=b))
    ends += so_far[1:]
    qkv, o, lse = attention(1, after(x2, *both), [w_all], [qkv, o, lse])
    ends = after(ends, lse)
    ffn_parts = both + both_other + ends + [swap(a, c=1) for a in ends]
    two = [[(kx, 0, 0) for kx in range(xs)], [(0, ky, kr) for ky in range(2)]]
    rest = [[(kx, 1, 0) for kx in range(xs)]]
    rest += [[(kx, ky, kr) for kx in range(b, 2 * b) for ky in range(2)] for b in bits(xs)]
    places = [
        [
            ((i * zs + kz) * kr, kr, kz, kx, ky, kc, part)
            for i, (kx, ky, part) in enumerate(units)
            for kz in range(zs)
        ]
        for group in (two, rest)
        for kc in range(2)
        for units in group
    ]

    tile = 512
    packet = ph + wh + per * ph
    steps, cp = 0, -(-nshard // 16) * 16
    block_out, dr, keep_f, send_f, wp_all, vec_f = pl.pallas_call(
        functools.partial(ffn_kernel, rps=rps, places=places, nslot=nshard),
        grid_spec=pltpu.PrefetchScalarGridSpec(
            num_scalar_prefetch=1,
            grid=(rows // tile,),
            in_specs=[
                row_spec(tile, width),
                row_spec(tile, width),
                row_spec(tile, width),
                all_spec(nshard * total, width),
            ]
            + [hbm] * len(ffn_parts),
            out_specs=[
                row_spec(tile, width),
                row_spec(tile, width),
                all_spec(width, packet),
                all_spec(width, packet),
                all_spec(width, width),
                all_spec(8, hidden),
            ],
            scratch_shapes=[
                pltpu.VMEM((width, width + 2 * hidden), BF),
                pltpu.VMEM((hidden, width), BF),
                pltpu.VMEM((width, hidden), F32),
                pltpu.VMEM((hidden, width), F32),
                pltpu.VMEM((width, width), F32),
                pltpu.SemaphoreType.DMA((sum(len(p) for p in places),)),
            ],
        ),
        out_shape=[
            jax.ShapeDtypeStruct((rows, width), F32),
            jax.ShapeDtypeStruct((rows, width), F32),
            jax.ShapeDtypeStruct((width, packet), BF),
            jax.ShapeDtypeStruct((width, packet), BF),
            jax.ShapeDtypeStruct((width, width), BF),
            jax.ShapeDtypeStruct((8, hidden), F32),
        ],
        compiler_params=params(58),
        cost_estimate=LITTLE,
        name="ffn",
    )(meta, o, x2, y2, slots, *ffn_parts)

    def add(parts, kind):
        total = parts[0].astype(F32)
        for p in parts[1:]:
            total = total + p.astype(F32)
        return total.astype(kind)

    def over_x(a):
        piece = lambda dx: lax.dynamic_slice_in_dim(a, (x + dx) % xs, 1, 1)
        return add([send(piece(dx), dx=dx) if dx else piece(0) for dx in range(xs)], BF)

    def over_y(a):
        n = a.shape[-1] // ys
        piece = lambda dy: lax.dynamic_slice_in_dim(a, (y + dy) % ys * n, n, a.ndim - 1)
        return add([send(piece(dy), dy=dy) if dy else piece(0) for dy in range(ys)], BF)

    def over_z(a):
        k = a.shape[0] // zs
        piece = lambda dz: lax.dynamic_slice_in_dim(a, (z + dz) % zs * k, k, 0)
        parts = [send(piece(dz), dz=dz) if dz else piece(0) for dz in range(zs)]
        return add(parts, BF)

    def over_xy(part):
        n = part.shape[1] // ys
        k = part.shape[0] // nshard
        view = part.reshape(zs, xs, k, ys * n)

        def corner(dx, dy):
            at = (0, (x + dx) % xs, 0, (y + dy) % ys * n)
            return lax.dynamic_slice(view, at, (zs, 1, k, n)).reshape(zs * k, n)

        parts = [
            send(corner(dx, dy), dx=dx, dy=dy) if dx or dy else corner(0, 0)
            for dx in range(xs)
            for dy in range(ys)
        ]
        return add(parts, BF)

    def replicas(part):
        found = {
            (dy, dc): send(part, dy=dy, dc=dc) if dy or dc else part
            for dy in range(ys)
            for dc in range(cs)
        }
        total = []
        for at in range(ys * cs):
            picked = jnp.zeros(part.shape, F32)
            for (dy, dc), piece in found.items():
                mine = ((y - dy + ys) % ys == at % ys) & ((core - dc + cs) % cs == at // ys)
                picked = jnp.where(mine, piece.astype(F32), picked)
            total.append(picked)
        return total

    steps = seq_count // seqs // calls

    def back(c, dr, before):
        nacc = width + 8
        sums = [all_spec(nacc, 3 * width)]
        halves = [all_spec(width, 3 * width // 2)] * 2 + [all_spec(8, width)]
        half_shapes = [
            jax.ShapeDtypeStruct((width, 3 * width // 2), BF),
            jax.ShapeDtypeStruct((width, 3 * width // 2), BF),
            jax.ShapeDtypeStruct((8, width), F32),
        ]
        return pl.pallas_call(
            functools.partial(back_kernel, seqs=seqs, span=span, begin=c == 0),
            grid_spec=pltpu.PrefetchScalarGridSpec(
                num_scalar_prefetch=1,
                grid=(steps,),
                in_specs=[
                    row_spec(seqs * span, width, c),
                    row_spec(seqs * span, width, c),
                    row_spec(seqs * span, 3 * width, c),
                    seq_spec(seqs, HEADS // 2, 2 * span, c),
                    all_spec(width, 3 * width),
                    all_spec(width, width),
                    all_spec(nshard * total, width),
                    seq_spec(seqs, 1, span, c),
                    seq_spec(seqs, nshard, span, c),
                ]
                + ((sums + [hbm, hbm]) if c else []),
                out_specs=[row_spec(seqs * span, 3 * width, c), seq_spec(seqs, cp, width, c)]
                + (halves if c else sums),
                scratch_shapes=([pltpu.VMEM((nacc, 3 * width), F32)] if c else [])
                + [pltpu.VMEM((seqs * cp, 2 * width), BF)],
            ),
            out_shape=[
                jax.ShapeDtypeStruct((rows, 3 * width), BF),
                jax.ShapeDtypeStruct((seq_count, cp, width), BF),
            ]
            + (half_shapes if c else [jax.ShapeDtypeStruct((nacc, 3 * width), F32)]),
            input_output_aliases={11: 0, 12: 1} if c else {},
            compiler_params=params(58),
            cost_estimate=LITTLE,
            name="back",
        )(meta, dr, x2, qkv, lse, w_all, wp_all, slots, doc_from, pbias, *before)

    dqkv, dpool, sums = back(0, dr, [])
    part_f = add([keep_f, after(send(send_f, dc=1), sums)], BF)
    dqkv, dpool, keep_a, send_a, vec_a = back(1, after(dr, part_f), [sums, dqkv, dpool])
    kf = part_f.shape[0] // nshard
    view = part_f.reshape(zs, xs, kf, packet)
    first_f = over_x(view[:, :, : kf // 2])
    second_f = over_y(view[:, :, kf // 2 :])

    dpool, keep_a = after((dpool, keep_a), first_f, second_f)
    part_a = add([keep_a, send(send_a, dc=1)], BF)
    part_f = jnp.concatenate([over_y(first_f), over_x(second_f)], axis=2)
    part_f = part_f.reshape(zs * kf, packet // ys)
    share_a = over_xy(part_a)
    share_f = over_z(part_f)
    grad_f = jnp.concatenate(replicas(share_f), axis=1)
    halves = [grad_f[:, i * packet : (i + 1) * packet] for i in range(2)]
    grad_project = jnp.concatenate([h[:, :ph] for h in halves], axis=1)
    grad_widen = jnp.concatenate([h[:, ph : ph + wh] for h in halves], axis=1)
    grad_narrow = jnp.concatenate(
        [
            jnp.concatenate(
                [h[:, ph + wh + j * ph : ph + wh + (j + 1) * ph] for h in halves], axis=1
            )
            for j in range(per)
        ],
        axis=0,
    )

    vec = jnp.concatenate(
        [vec_f[0].reshape(per, width), vec_f[1:2, :width], vec_a[:2], vec_f[2:4, :width]], axis=0
    ).astype(BF)
    nvec = vec.shape[0]
    dp = jnp.transpose(dpool[:, :nshard], (1, 0, 2)).reshape(xs, zs, seq_count, width)
    dp = jnp.concatenate([dp, jnp.broadcast_to(vec, (xs, zs, nvec, width))], axis=2)
    for b in reversed(bits(xs)):
        dp = add([dp[:b], swap(dp[b:], x=b)], BF)
    dp = dp[0]
    for b in reversed(bits(zs)):
        dp = add([dp[:b], swap(dp[b:], z=b)], BF)
    own = dp[0].astype(F32)
    own_vec = jnp.concatenate(
        [lax.dynamic_slice(own[seq_count:].reshape(nvec * width), (shard * hs,), (hs,))]
        + [
            lax.dynamic_slice(own[seq_count + per + i], (shard * rps,), (rps,))
            for i in range(5)
        ]
    ).astype(BF)
    tokens_grad = pl.pallas_call(
        functools.partial(last_kernel, seqs=seqs, span=span, nslot=nshard),
        grid=(seq_count // seqs,),
        in_specs=[
            smem,
            smem,
            pl.BlockSpec((seqs * span, width), lambda i: (i, 0)),
            pl.BlockSpec((seqs * span, width), lambda i: (i, 0)),
            pl.BlockSpec((seqs * span, 3 * width), lambda i: (i, 0)),
            pl.BlockSpec((width, 3 * width), lambda i: (0, 0)),
            pl.BlockSpec((seqs, 1, width), lambda i: (i, 0, 0)),
            pl.BlockSpec((nshard * total, width), lambda i: (0, 0)),
        ],
        out_specs=pl.BlockSpec((seqs * span, width), lambda i: (i, 0)),
        out_shape=jax.ShapeDtypeStruct((rows, width), F32),
        compiler_params=params(58),
        cost_estimate=LITTLE,
        name="last",
    )(
        meta,
        doc_lengths,
        after(dr, part_a),
        x2,
        dqkv,
        w_all,
        own[:seq_count].reshape(seq_count, 1, width),
        slots,
    )

    share_a = over_z(share_a)
    ncol = share_a.shape[1]
    vrows = -(-own_vec.shape[0] // ncol)
    own_vec = jnp.pad(own_vec, (0, vrows * ncol - own_vec.shape[0])).reshape(vrows, ncol)
    found = replicas(jnp.concatenate([share_a, own_vec], axis=0))
    grad_attend = jnp.concatenate([f[:rps] for f in found], axis=1)
    vec = sum(f[rps:] for f in found).reshape(vrows * ncol)
    vecs = [vec[:hs]] + [vec[hs + i * rps : hs + (i + 1) * rps] for i in range(5)]
    return (
        block_out.reshape(tokens.shape),
        tokens_grad.reshape(tokens.shape),
        grad_attend,
        grad_project,
        grad_widen,
        grad_narrow,
        *vecs,
    )


def solution(mesh):
    first = mesh.devices[0]
    xs = len({d.coords[0] for d in first})
    cs = len({d.core_on_chip for d in mesh.devices[:, 0]})
    sizes = (mesh.shape["shard"] // xs, xs, mesh.shape["rep"] // cs, cs)
    row = P("shard", None)
    vec = P("shard")
    act = P("rep", "shard", None)
    return jax.shard_map(
        functools.partial(local, sizes=sizes),
        mesh=mesh,
        in_specs=(act, act, P("rep", None), row, row, row, row) + (vec,) * 6,
        out_specs=(act, act, row, row, row, row) + (vec,) * 6,
        check_vma=False,
    )
```
